512 devices in a mesh: dm: 16 (over z, core), hv: 32 (over y, x).
Axes of the slice: x: 4, y: 8, z: 8, core: 2. Of those that a mesh axis runs over, the one named last changes fastest.
Arguments:
- tokens: bfloat16 [512, 16384], P('hv', 'dm'), may hold values from -64 to 64
- gate_weight: bfloat16 [16384, 13312], P('dm', 'hv'), may hold values from -0.046875 to 0.046875
- up_weight: bfloat16 [16384, 13312], P('dm', 'hv'), may hold values from -0.046875 to 0.046875
- down_weight: bfloat16 [13312, 16384], P('hv', 'dm'), may hold values from -0.0546875 to 0.0546875
- norm_gain: float32 [16384], P('dm'), may hold values from 0.1 to 1.9
- unembed: bfloat16 [16384, 32064], P('dm', 'hv'), may hold values from -8 to 8
- gold_ids: int32 [512], replicated, may hold values from 0 to 32063
- option_lengths: int32 [32], replicated, may hold values from 1 to 32, 512 in all
Outputs:
- token_logprob: float32 [512], replicated
- option_score: float32 [32], replicated
The draws below stay inside these ranges and needn't reach their ends.
All inputs are finite; a program needn't handle non-finite values.
Results may differ from the reference program's by a relative error of at most 0.005.
Values may be sent and summed in bfloat16 or wider, within the bound.
A program may use at most 64 MiB of HBM per device.

```python
import math
import jax
import jax.numpy as jnp
import numpy as np
from jax import lax

D = 16384
FF = 13312
V = 32064
TOKENS = 512
MOST = 32
NOPT = 32


def draw_tokens(key, part):
    first, second, third = jax.random.split(key, 3)
    column = jnp.exp(jnp.arange(D, dtype=jnp.float32) * (math.log(3.0) / D))
    column = column * jnp.exp(jax.random.uniform(second, (D,), jnp.float32, -0.7, 0.7))
    base = jnp.clip(jax.random.normal(first, (TOKENS, D), jnp.float32), -4.0, 4.0)
    rowscale = jnp.exp(jax.random.uniform(third, (TOKENS, 1), jnp.float32, 0.0, math.log(4.0)))
    return (0.5 * base * rowscale * column).astype(jnp.bfloat16)


def draw_unembed(key, part):
    first = jax.random.fold_in(key, 0)
    base = jnp.clip(jax.random.normal(first, (D, V), jnp.float32), -4.0, 4.0)
    values = base * (3.0 / math.sqrt(D))
    return jnp.clip(values, -8.0, 8.0).astype(jnp.bfloat16)


def set_ends(values, own_key, least, high):
    extent = values.shape
    spot = [jax.random.randint(jax.random.fold_in(own_key, axis), (), 0, extent[axis]) for axis in range(len(extent))]
    values = values.at[tuple(spot)].set(least)
    longest = extent.index(max(extent))
    spot[longest] = (spot[longest] + 1) % extent[longest]
    return values.at[tuple(spot)].set(high)


def shard_levels(rng, shape, cuts, least, high):
    def one(position, shards_of):
        heights = jax.random.uniform(jax.random.fold_in(jax.random.fold_in(rng, 6), position), (shards_of,), jnp.float32, least / len(cuts), high / len(cuts))
        return jnp.repeat(jnp.exp(heights), shape[position] // shards_of).reshape((-1,) + (1,) * (len(shape) - position - 1))

    factor_of = one(*cuts[0])
    for cut in cuts[1:]:
        factor_of = factor_of * one(*cut)
    return factor_of


def split_up(count, total, reach, lean):
    loads = [(1 << 20) // math.isqrt(rank ** lean) + 1 for rank in range(2, count + 1)]
    spare, holding = total - reach - (count - 1), [1] * (count - 1)
    while spare > 0:
        candidates = [i for i in range(count - 1) if holding[i] < reach]
        mass, budget = sum([loads[i] for i in candidates]), spare
        for i in candidates:
            extra = min(reach - holding[i], max(1, budget * loads[i] // mass), spare)
            holding[i] = holding[i] + extra
            spare = spare - extra
    return np.array([reach] + holding)


def uneven(own_key, amount, total, most, lean):
    if amount == 2:
        one = jax.random.randint(own_key, (), max(1, total - most), min(most, total - 1) + 1)
        return jnp.stack([one, total - one])
    sizes = jnp.asarray(split_up(amount, total, most, lean), jnp.int32)
    pairs = (amount - 1) // 2
    donor, sink = sizes[1:1 + 2 * pairs:2], sizes[2:2 + 2 * pairs:2]
    margin = jnp.minimum(donor - 1, most - sink)
    passed = jax.random.randint(jax.random.fold_in(own_key, 1), (pairs,), 0, 1 << 20) % (margin + 1)
    sizes = sizes.at[1:1 + 2 * pairs:2].set(donor - passed).at[2:2 + 2 * pairs:2].set(sink + passed)
    return sizes[jax.random.permutation(jax.random.fold_in(own_key, 2), amount)]


def bell_draw(stream_key, extent, scale, most, shards=(), held_as=jnp.bfloat16):
    gain = shard_levels(stream_key, extent, shards, -0.22, 0.18) if shards else 1.0
    array = jax.random.normal(stream_key, extent, jnp.float32) * scale * gain
    return jnp.minimum(jnp.maximum(array, -most), most).astype(held_as)


def setup_inputs(seed: int = 0) -> dict:
    streams_of = jax.random.split(jax.random.key(seed), 9)
    return {
        "tokens": draw_tokens(jax.random.fold_in(streams_of[8], 71), 0),
        "gate_weight": bell_draw(streams_of[1], (D, FF), D ** -0.5, 0.046875, ((0, 16), (1, 32))),
        "up_weight": bell_draw(streams_of[2], (D, FF), D ** -0.5, 0.046875, ((0, 16), (1, 32))),
        "down_weight": bell_draw(streams_of[3], (FF, D), FF ** -0.5, 0.0546875, ((0, 32), (1, 16))),
        "norm_gain": jnp.clip(1.0 + 0.18 * jax.random.normal(streams_of[4], (D,), jnp.float32), 0.1, 1.9),
        "unembed": draw_unembed(jax.random.fold_in(streams_of[8], 71), 0),
        "gold_ids": set_ends(jax.random.randint(streams_of[6], (TOKENS,), 0, V), jax.random.fold_in(streams_of[6], 1), 0, V - 1).astype(jnp.int32),
        "option_lengths": uneven(streams_of[7], NOPT, TOKENS, MOST, 1).astype(jnp.int32),
    }


def reference(tokens, gate_weight, up_weight, down_weight, norm_gain, unembed, gold_ids, option_lengths):
    gate = jnp.dot(tokens, gate_weight, preferred_element_type=jnp.float32)
    up = jnp.dot(tokens, up_weight, preferred_element_type=jnp.float32)
    hidden = (jax.nn.silu(gate) * up).astype(jnp.bfloat16)
    ffn = jnp.dot(hidden, down_weight, preferred_element_type=jnp.float32)
    resid = (tokens.astype(jnp.float32) + ffn).astype(jnp.bfloat16)
    wide = resid.astype(jnp.float32)
    squares = lax.optimization_barrier(jnp.sum(wide * wide, axis=1, keepdims=True))
    normed = (wide * lax.rsqrt(squares / D + 1e-05) * norm_gain).astype(jnp.bfloat16)
    logits = jnp.dot(normed, unembed, preferred_element_type=jnp.float32)
    top = lax.optimization_barrier(jnp.max(logits, axis=1))
    total = lax.optimization_barrier(jnp.sum(jnp.exp(logits - top[:, None]), axis=1))
    gold = jnp.take_along_axis(logits, gold_ids[:, None].astype(jnp.int32), axis=1)[:, 0]
    token_logprob = gold - top - jnp.log(total)
    ends = jnp.cumsum(option_lengths)
    starts = ends - option_lengths
    places = jnp.arange(TOKENS, dtype=jnp.int32)
    member = ((places[None, :] >= starts[:, None]) & (places[None, :] < ends[:, None])).astype(jnp.float32)
    summed = jnp.dot(member, token_logprob, precision=lax.Precision.HIGHEST)
    option_score = summed / option_lengths.astype(jnp.float32)
    return (token_logprob, option_score)
```

```python
import jax
import jax.numpy as jnp
from jax import lax
from jax.experimental import pallas as pl
from jax.experimental.pallas import tpu as pltpu
from jax.sharding import PartitionSpec as P

D = 16384
NZ, NC, NY, NX = 8, 2, 8, 4
ROWS = 16
WIDE = 1024
FF = 416
VOC = 1002
VPAD = 1024
CA = 256
CB = WIDE - CA
OWN = 32
FAR8 = (4, 3, 5, 2, 6, 1, 7)
FAR4 = (2, 1, 3)
LOW = -1e30
COPIES = 128
MESH = pl.DeviceIdType.MESH
BF = jnp.bfloat16
F32 = jnp.float32
NT = (((1,), (1,)), ((), ()))


def kernel(
    tok, wg, wu, wd, gain, un, gold, lens, lp_out, score_out,
    w_in, w_down, w_un, xa, xb, s1, r1, p1, s2, r2, hid,
    qa, qb, ra, rb, ta, tb, ra2, rb2, res, ya, yb,
    s3, r3, p3, s4, r4, st1, st2, st3, send_sem, recv_sem, local_sem,
):
    dm = lax.axis_index("dm")
    hv = lax.axis_index("hv")
    z, c = dm // NC, lax.rem(dm, NC)
    y, x = hv // NX, lax.rem(hv, NX)
    oc = 1 - c

    def at(zz=None, cc=None, yy=None, xx=None):
        zz = z if zz is None else zz
        cc = c if cc is None else cc
        yy = y if yy is None else yy
        xx = x if xx is None else xx
        return (zz * NC + cc, yy * NX + xx)

    def up(v, k, n):
        return lax.rem(v + k, n)

    loads = [
        pltpu.make_async_copy(wg, w_in.at[pl.ds(0, FF)], local_sem.at[0]),
        pltpu.make_async_copy(wu, w_in.at[pl.ds(FF, FF)], local_sem.at[1]),
        pltpu.make_async_copy(wd, w_down, local_sem.at[2]),
    ]
    for load in loads:
        load.start()

    barrier = pltpu.get_barrier_semaphore()
    greet = (
        [at(yy=up(y, k, NY)) for k in FAR8]
        + [at(zz=up(z, k, NZ)) for k in FAR8]
        + [at(xx=up(x, k, NX)) for k in FAR4]
        + [at(cc=oc)]
        + [at(cc=oc, xx=up(x, k, NX)) for k in FAR4]
    )
    for peer in greet:
        pl.semaphore_signal(barrier, inc=1, device_id=peer, device_id_type=MESH)
    pl.semaphore_wait(barrier, len(greet))

    count = [0]
    pending = []

    def send(src, dst, peer):
        n = count[0]
        count[0] = n + 1
        copy = pltpu.make_async_remote_copy(
            src_ref=src,
            dst_ref=dst,
            send_sem=send_sem.at[n],
            recv_sem=recv_sem.at[n],
            device_id=peer,
            device_id_type=MESH,
        )
        copy.start()
        pending.append(copy)
        return copy

    def sent():
        for copy in pending:
            copy.wait_send()
        pending.clear()

    def gather_hv(block, ga, gb):
        mine_a = block.at[:, pl.ds(0, CA)]
        mine_b = block.at[:, pl.ds(CA, CB)]
        first_b = [send(mine_b, gb.at[y, x], at(yy=up(y, k, NY))) for k in FAR8]
        first_a = [send(mine_a, ga.at[y, x], at(xx=up(x, k, NX))) for k in FAR4]
        ga[y, x] = block[:, :CA]
        gb[y, x] = block[:, CA:]
        for copy in first_a:
            copy.wait_recv()
        last = [send(ga.at[y], ga.at[y], at(yy=up(y, k, NY))) for k in FAR8]
        for copy in first_b:
            copy.wait_recv()
        last += [send(gb.at[:, x], gb.at[:, x], at(xx=up(x, k, NX))) for k in FAR4]
        return last

    def part(ga, gb, cc):
        n = NY * 2 * ROWS
        a = ga[:, pl.ds(2 * cc, 2)].reshape(n, CA)
        b = gb[:, pl.ds(2 * cc, 2)].reshape(n, CB)
        return a, b

    def product(a, b, w):
        return lax.dot_general(
            a, w[:, :CA], NT, preferred_element_type=F32
        ) + lax.dot_general(b, w[:, CA:], NT, preferred_element_type=F32)

    def scatter_dm(make, mine, out, got, out2, got2):
        out[...] = make(oc).astype(BF)
        swap = send(out, got, at(cc=oc))
        mine[...] = make(c)
        swap.wait_recv()
        out2[...] = (mine[...] + got[...].astype(F32)).astype(BF)
        copies = [
            send(out2.at[up(z, k, NZ)], got2.at[i], at(zz=up(z, k, NZ)))
            for i, k in enumerate(FAR8)
        ]
        total = mine[z] + got[z].astype(F32)
        sent_before = pending[: -len(copies)]
        for copy in sent_before:
            copy.wait_send()
        del pending[: -len(copies)]
        for i, copy in reversed(list(enumerate(copies))):
            copy.wait_recv()
            total = total + got2[i].astype(F32)
        return total

    last = gather_hv(tok, xa, xb)

    g = gain[...]
    step = 32

    def fold(i, carry):
        rows = pl.ds(pl.multiple_of(i * step, step), step)
        w_un[rows, :] = (un[rows, :].astype(F32) * g).astype(BF)
        return carry

    whole = VOC // step
    lax.fori_loop(0, whole, fold, 0)
    w_un[whole * step :, :] = jnp.zeros((VPAD - whole * step, WIDE), BF)
    w_un[whole * step : VOC, :] = (un[whole * step :, :].astype(F32) * g).astype(BF)

    loads[0].wait()
    loads[1].wait()
    loads[2].wait()
    for copy in last:
        copy.wait_recv()

    w_first = w_in[...]

    def gate_up(cc):
        a, b = part(xa, xb, cc)
        return product(a, b, w_first).reshape(NZ, OWN, 2 * FF)

    total = scatter_dm(gate_up, p1, s1, r1, s2, r2)
    gate, upper = total[:, :FF], total[:, FF:]
    hid[z, c] = (gate / (1.0 + jnp.exp(-gate)) * upper).astype(BF)

    far = [send(hid.at[z, c], hid.at[z, c], at(zz=up(z, k, NZ))) for k in FAR8]
    near = [send(hid.at[z, c], hid.at[z, c], at(cc=oc))]
    for k, copy in reversed(list(zip(FAR8, far))):
        copy.wait_recv()
        origin = up(z, NZ - k, NZ)
        near.append(send(hid.at[origin, c], hid.at[origin, c], at(cc=oc)))
    for copy in near:
        copy.wait_recv()

    h = hid[...].reshape(NZ * NC * OWN, FF)
    q = jnp.dot(h, w_down[...], preferred_element_type=F32).astype(BF)
    qb[...] = q[:, CA:].reshape(NY, NX, ROWS, CB)
    qa[...] = q[:, :CA].reshape(NY, NX, ROWS, CA)
    first_b = [
        send(qb.at[:, up(x, k, NX)], rb.at[i], at(xx=up(x, k, NX)))
        for i, k in enumerate(FAR4)
    ]
    first_a = [
        send(qa.at[up(y, k, NY)], ra.at[i], at(yy=up(y, k, NY)))
        for i, k in enumerate(FAR8)
    ]
    sum_b = qb[:, x].astype(F32)
    for i, copy in reversed(list(enumerate(first_b))):
        copy.wait_recv()
        sum_b = sum_b + rb[i].astype(F32)
    tb[...] = sum_b.astype(BF)
    last_b = [
        send(tb.at[up(y, k, NY)], rb2.at[i], at(yy=up(y, k, NY)))
        for i, k in enumerate(FAR8)
    ]
    sum_a = qa[y].astype(F32)
    for i, copy in reversed(list(enumerate(first_a))):
        copy.wait_recv()
        sum_a = sum_a + ra[i].astype(F32)
    ta[...] = sum_a.astype(BF)
    last_a = [
        send(ta.at[up(x, k, NX)], ra2.at[i], at(xx=up(x, k, NX)))
        for i, k in enumerate(FAR4)
    ]
    res_a = tok[:, :CA].astype(F32) + ta[x].astype(F32)
    res_b = tok[:, CA:].astype(F32) + tb[y].astype(F32)
    for i, copy in reversed(list(enumerate(last_a))):
        copy.wait_recv()
        res_a = res_a + ra2[i].astype(F32)
    for i, copy in reversed(list(enumerate(last_b))):
        copy.wait_recv()
        res_b = res_b + rb2[i].astype(F32)
    res[:, :CA] = res_a.astype(BF)
    res[:, CA:] = res_b.astype(BF)

    last = gather_hv(res, ya, yb)
    for copy in last:
        copy.wait_recv()
    w_last = w_un[...]

    def logit_part(cc):
        a, b = part(ya, yb, cc)
        out = product(a, b, w_last)
        wide_a, wide_b = a.astype(F32), b.astype(F32)
        ss = jnp.sum(wide_a * wide_a, axis=1, keepdims=True) + jnp.sum(
            wide_b * wide_b, axis=1, keepdims=True
        )
        high = ss.astype(BF).astype(F32)
        tail = out[:, VPAD - 128 :]
        lane = lax.broadcasted_iota(jnp.int32, tail.shape, 1) + (VPAD - 128)
        tail = jnp.where(lane == VOC, high, jnp.where(lane == VOC + 1, ss - high, tail))
        out = jnp.concatenate([out[:, : VPAD - 128], tail], axis=1)
        return out.reshape(NZ, OWN, VPAD)

    total = scatter_dm(logit_part, p3, s3, r3, s4, r4)

    lane = lax.broadcasted_iota(jnp.int32, (OWN, VPAD), 1)
    ss = jnp.sum(
        jnp.where((lane == VOC) | (lane == VOC + 1), total, 0.0), axis=1, keepdims=True
    )
    logits = total * lax.rsqrt(ss / D + 1e-05)
    inside = lane < VOC
    top = jnp.max(jnp.where(inside, logits, LOW), axis=1, keepdims=True)
    mass = jnp.sum(jnp.where(inside, jnp.exp(logits - top), 0.0), axis=1, keepdims=True)
    place = lax.rem(dm, 4) * OWN
    row = lax.broadcasted_iota(jnp.int32, (OWN, 128), 0)
    col = lax.broadcasted_iota(jnp.int32, (OWN, 128), 1)
    diag = col == row + place
    ids = gold[pl.ds(dm // 4, 1), :].astype(F32)
    wanted = jnp.sum(jnp.where(diag, ids, 0.0), axis=1, keepdims=True).astype(jnp.int32)
    hit = inside & (lane + hv * VOC == wanted)
    found = jnp.sum(jnp.where(hit, logits, 0.0), axis=1, keepdims=True)

    def flat(v, other):
        return jnp.max(jnp.where(diag, v, other), axis=0, keepdims=True)

    def flat_sum(v):
        return jnp.sum(jnp.where(diag, v, 0.0), axis=0, keepdims=True)

    def pack(t, m, f):
        line = lax.broadcasted_iota(jnp.int32, (8, 128), 0)
        return jnp.where(line == 0, t, jnp.where(line == 1, m, jnp.where(line == 2, f, 0.0)))

    def combine(tiles):
        best = tiles[0][0:1]
        for t in tiles[1:]:
            best = jnp.maximum(best, t[0:1])
        m = jnp.zeros((1, 128), F32)
        f = jnp.zeros((1, 128), F32)
        for t in tiles:
            m = m + t[1:2] * jnp.exp(t[0:1] - best)
            f = f + t[2:3]
        return best, m, f

    st1[0] = pack(flat(top, LOW), flat_sum(mass), flat_sum(found))
    copies = [send(st1.at[0], st1.at[1], at(cc=oc))]
    for i, k in enumerate(FAR4):
        copies.append(send(st1.at[0], st1.at[2 + 2 * i], at(xx=up(x, k, NX))))
        copies.append(send(st1.at[0], st1.at[3 + 2 * i], at(cc=oc, xx=up(x, k, NX))))
    for copy in copies:
        copy.wait_recv()
    st2[0] = pack(*combine([st1[i] for i in range(8)]))
    copies = [
        send(st2.at[0], st2.at[1 + i], at(yy=up(y, k, NY))) for i, k in enumerate(FAR8)
    ]
    amount = lens[...].astype(F32)
    one = lax.broadcasted_iota(jnp.int32, (OWN, OWN), 0)
    two = lax.broadcasted_iota(jnp.int32, (OWN, OWN), 1)
    ends = jnp.sum(jnp.where(two <= one, amount, 0.0), axis=1, keepdims=True)
    length = jnp.sum(jnp.where(two == one, amount, 0.0), axis=1, keepdims=True)
    starts = ends - length
    for copy in copies:
        copy.wait_recv()
    best, m, f = combine([st2[i] for i in range(8)])
    spot = lax.broadcasted_iota(jnp.int32, (1, 128), 1)
    base = lax.rem(z, 2) * 2 * OWN
    valid = (spot >= base) & (spot < base + 2 * OWN)
    value = jnp.where(valid, f - best - jnp.log(jnp.where(valid, m, 1.0)), 0.0)
    st3[z] = jnp.broadcast_to(value, (8, 128))
    copies = [send(st3.at[z], st3.at[z], at(zz=up(z, k, NZ))) for k in FAR8]
    for copy in copies:
        copy.wait_recv()
    acc = jnp.zeros((OWN, 1), F32)
    for i in range(4):
        line = st3[2 * i][0:1] + st3[2 * i + 1][0:1]
        lp_out[i : i + 1, :] = line
        where = (col + 128 * i).astype(F32)
        member = (where >= starts) & (where < ends)
        acc = acc + jnp.sum(jnp.where(member, line, 0.0), axis=1, keepdims=True)
    score = acc / length
    score_out[...] = jnp.sum(jnp.where(two == one, score, 0.0), axis=0, keepdims=True)
    sent()


def per_device(
    tokens, gate_weight, up_weight, down_weight, norm_gain, unembed, gold_ids, option_lengths
):
    vm = pl.BlockSpec(memory_space=pltpu.VMEM)
    anyspace = pl.BlockSpec(memory_space=pl.ANY)
    scratch = [
        pltpu.VMEM((2 * FF, WIDE), BF),
        pltpu.VMEM((FF, WIDE), BF),
        pltpu.VMEM((VPAD, WIDE), BF),
        pltpu.VMEM((NY, NX, ROWS, CA), BF),
        pltpu.VMEM((NY, NX, ROWS, CB), BF),
        pltpu.VMEM((NZ, OWN, 2 * FF), BF),
        pltpu.VMEM((NZ, OWN, 2 * FF), BF),
        pltpu.VMEM((NZ, OWN, 2 * FF), F32),
        pltpu.VMEM((NZ, OWN, 2 * FF), BF),
        pltpu.VMEM((NZ - 1, OWN, 2 * FF), BF),
        pltpu.VMEM((NZ, NC, OWN, FF), BF),
        pltpu.VMEM((NY, NX, ROWS, CA), BF),
        pltpu.VMEM((NY, NX, ROWS, CB), BF),
        pltpu.VMEM((NY - 1, NX, ROWS, CA), BF),
        pltpu.VMEM((NX - 1, NY, ROWS, CB), BF),
        pltpu.VMEM((NX, ROWS, CA), BF),
        pltpu.VMEM((NY, ROWS, CB), BF),
        pltpu.VMEM((NX - 1, ROWS, CA), BF),
        pltpu.VMEM((NY - 1, ROWS, CB), BF),
        pltpu.VMEM((ROWS, WIDE), BF),
        pltpu.VMEM((NY, NX, ROWS, CA), BF),
        pltpu.VMEM((NY, NX, ROWS, CB), BF),
        pltpu.VMEM((NZ, OWN, VPAD), BF),
        pltpu.VMEM((NZ, OWN, VPAD), BF),
        pltpu.VMEM((NZ, OWN, VPAD), F32),
        pltpu.VMEM((NZ, OWN, VPAD), BF),
        pltpu.VMEM((NZ - 1, OWN, VPAD), BF),
        pltpu.VMEM((8, 8, 128), F32),
        pltpu.VMEM((8, 8, 128), F32),
        pltpu.VMEM((8, 8, 128), F32),
        pltpu.SemaphoreType.DMA((COPIES,)),
        pltpu.SemaphoreType.DMA((COPIES,)),
        pltpu.SemaphoreType.DMA((4,)),
    ]
    logprob, score = pl.pallas_call(
        kernel,
        out_shape=(
            jax.ShapeDtypeStruct((4, 128), F32),
            jax.ShapeDtypeStruct((1, OWN), F32),
        ),
        in_specs=[vm, anyspace, anyspace, anyspace, vm, vm, vm, vm],
        out_specs=(vm, vm),
        scratch_shapes=scratch,
        name="score",
        compiler_params=pltpu.CompilerParams(
            collective_id=0, has_side_effects=True, vmem_limit_bytes=56 << 20
        ),
    )(
        tokens,
        gate_weight.T,
        up_weight.T,
        down_weight,
        norm_gain.reshape(1, WIDE),
        unembed.T,
        gold_ids.reshape(4, 128),
        option_lengths.reshape(1, OWN),
    )
    return logprob.reshape(512), score.reshape(OWN)


def solution(mesh):
    placed = (
        P("hv", "dm"),
        P("dm", "hv"),
        P("dm", "hv"),
        P("hv", "dm"),
        P("dm"),
        P("dm", "hv"),
        P(),
        P(),
    )
    return jax.shard_map(
        per_device, mesh=mesh, in_specs=placed, out_specs=(P(), P()), check_vma=False
    )
```

```python
import jax
import jax.numpy as jnp
from jax import lax
from jax.experimental import pallas as pl
from jax.experimental.pallas import tpu as pltpu
from jax.sharding import PartitionSpec as P

D = 16384
NZ, NC, NY, NX = 8, 2, 8, 4
ROWS = 16
WIDE = 1024
FF = 416
VOC = 1002
VPAD = 1024
CA = 384
CB = WIDE - CA
NH = 2
RH = ROWS // NH
OWN = 2 * RH
NOPT = 32
FAR8 = (4, 3, 5, 2, 6, 1, 7)
FAR4 = (2, 1, 3)
LOW = -1e30
COPIES = 240
MESH = pl.DeviceIdType.MESH
BF = jnp.bfloat16
F32 = jnp.float32
NT = (((1,), (1,)), ((), ()))


def kernel(
    tok, wg, wu, wd, gain, un, gold, lens, lp_out, score_out,
    w_in, w_down, w_raw, w_un, xa, xb, s1, r1, p1, s2, r2, hid,
    qa, qb, ra, rb, ta, tb, ra2, rb2, res, ya, yb,
    s3, r3, p3, s4, r4, st1, st2, st3, send_sem, recv_sem, local_sem,
):
    dm = lax.axis_index("dm")
    hv = lax.axis_index("hv")
    z, c = dm // NC, lax.rem(dm, NC)
    y, x = hv // NX, lax.rem(hv, NX)
    oc = 1 - c

    def at(zz=None, cc=None, yy=None, xx=None):
        zz = z if zz is None else zz
        cc = c if cc is None else cc
        yy = y if yy is None else yy
        xx = x if xx is None else xx
        return (zz * NC + cc, yy * NX + xx)

    def up(v, k, n):
        return lax.rem(v + k, n)

    loads = [
        pltpu.make_async_copy(wg, w_in.at[pl.ds(0, FF)], local_sem.at[0]),
        pltpu.make_async_copy(wu, w_in.at[pl.ds(FF, FF)], local_sem.at[1]),
        pltpu.make_async_copy(wd, w_down, local_sem.at[2]),
        pltpu.make_async_copy(un, w_raw, local_sem.at[3]),
    ]
    for load in loads:
        load.start()

    barrier = pltpu.get_barrier_semaphore()
    greet = (
        [at(yy=up(y, k, NY)) for k in FAR8]
        + [at(zz=up(z, k, NZ)) for k in FAR8]
        + [at(xx=up(x, k, NX)) for k in FAR4]
        + [at(cc=oc)]
        + [at(cc=oc, xx=up(x, k, NX)) for k in FAR4]
    )
    for peer in greet:
        pl.semaphore_signal(barrier, inc=1, device_id=peer, device_id_type=MESH)
    pl.semaphore_wait(barrier, len(greet))

    count = [0]
    pending = []

    def send(src, dst, peer):
        n = count[0]
        count[0] = n + 1
        copy = pltpu.make_async_remote_copy(
            src_ref=src,
            dst_ref=dst,
            send_sem=send_sem.at[n],
            recv_sem=recv_sem.at[n],
            device_id=peer,
            device_id_type=MESH,
        )
        copy.start()
        pending.append(copy)
        return copy

    def sent():
        for copy in pending:
            copy.wait_send()
        pending.clear()

    def arrive(copies):
        for copy in copies:
            copy.wait_recv()

    def gather_hv(block_a, block_b, ga, gb):
        first_b = [send(block_b, gb.at[y, x], at(yy=up(y, k, NY))) for k in FAR8]
        first_a = [send(block_a, ga.at[y, x], at(xx=up(x, k, NX))) for k in FAR4]
        ga[y, x] = block_a[...]
        gb[y, x] = block_b[...]
        yield
        arrive(first_a)
        last = [send(ga.at[y], ga.at[y], at(yy=up(y, k, NY))) for k in FAR8]
        arrive(first_b)
        last += [send(gb.at[:, x], gb.at[:, x], at(xx=up(x, k, NX))) for k in FAR4]
        yield
        arrive(last)

    def part(ga, gb, cc):
        n = NY * 2 * RH
        a = ga[:, pl.ds(2 * cc, 2)].reshape(n, CA)
        b = gb[:, pl.ds(2 * cc, 2)].reshape(n, CB)
        return a, b

    def product(a, b, w):
        return lax.dot_general(
            a, w[:, :CA], NT, preferred_element_type=F32
        ) + lax.dot_general(b, w[:, CA:], NT, preferred_element_type=F32)

    def scatter_dm(make, mine, out, got, out2, got2, done):
        out[...] = make(oc).astype(BF)
        swap = send(out, got, at(cc=oc))
        mine[...] = make(c)
        arrive([swap])
        out2[...] = (mine[...] + got[...].astype(F32)).astype(BF)
        copies = [
            send(out2.at[up(z, k, NZ)], got2.at[i], at(zz=up(z, k, NZ)))
            for i, k in enumerate(FAR8)
        ]
        total = mine[z] + got[z].astype(F32)
        yield
        for i, copy in reversed(list(enumerate(copies))):
            arrive([copy])
            total = total + got2[i].astype(F32)
        done.append(total)

    def gate_up(cc, h):
        a, b = part(xa.at[h], xb.at[h], cc)
        return product(a, b, w_in[...]).reshape(NZ, OWN, 2 * FF)

    def logit_part(cc, h):
        a, b = part(ya.at[h], yb.at[h], cc)
        out = product(a, b, w_un[...])
        wide_a, wide_b = a.astype(F32), b.astype(F32)
        ss = jnp.sum(wide_a * wide_a, axis=1, keepdims=True) + jnp.sum(
            wide_b * wide_b, axis=1, keepdims=True
        )
        high = ss.astype(BF).astype(F32)
        tail = out[:, VPAD - 128 :]
        lane = lax.broadcasted_iota(jnp.int32, tail.shape, 1) + (VPAD - 128)
        tail = jnp.where(lane == VOC, high, jnp.where(lane == VOC + 1, ss - high, tail))
        out = jnp.concatenate([out[:, : VPAD - 128], tail], axis=1)
        return out.reshape(NZ, OWN, VPAD)

    def half(h, result):
        rows = pl.ds(h * RH, RH)
        yield from gather_hv(
            tok.at[rows, pl.ds(0, CA)], tok.at[rows, pl.ds(CA, CB)], xa.at[h], xb.at[h]
        )
        if h == 0:
            loads[0].wait()
            loads[1].wait()
            loads[2].wait()
        done = []
        yield from scatter_dm(
            lambda cc: gate_up(cc, h), p1.at[h], s1.at[h], r1.at[h], s2.at[h], r2.at[h], done
        )
        gate, upper = done[0][:, :FF], done[0][:, FF:]
        mine = hid.at[h]
        mine[z, c] = (gate / (1.0 + jnp.exp(-gate)) * upper).astype(BF)

        far = [send(mine.at[z, c], mine.at[z, c], at(zz=up(z, k, NZ))) for k in FAR8]
        near = [send(mine.at[z, c], mine.at[z, c], at(cc=oc))]
        yield
        for k, copy in reversed(list(zip(FAR8, far))):
            arrive([copy])
            origin = up(z, NZ - k, NZ)
            near.append(send(mine.at[origin, c], mine.at[origin, c], at(cc=oc)))
        arrive(near)

        q = jnp.dot(
            mine[...].reshape(NZ * NC * OWN, FF), w_down[...], preferred_element_type=F32
        )
        q = q.reshape(NY, NX, RH, WIDE).astype(BF)
        qb[h] = q[..., CA:]
        first_b = [
            send(qb.at[h, :, up(x, k, NX)], rb.at[h, i], at(xx=up(x, k, NX)))
            for i, k in enumerate(FAR4)
        ]
        qa[h] = q[..., :CA]
        first_a = [
            send(qa.at[h, up(y, k, NY)], ra.at[h, i], at(yy=up(y, k, NY)))
            for i, k in enumerate(FAR8)
        ]
        yield
        sum_b = qb[h, :, x].astype(F32)
        for i, copy in reversed(list(enumerate(first_b))):
            arrive([copy])
            sum_b = sum_b + rb[h, i].astype(F32)
        tb[h] = sum_b.astype(BF)
        last_b = [
            send(tb.at[h, up(y, k, NY)], rb2.at[h, i], at(yy=up(y, k, NY)))
            for i, k in enumerate(FAR8)
        ]
        sum_a = qa[h, y].astype(F32)
        for i, copy in reversed(list(enumerate(first_a))):
            arrive([copy])
            sum_a = sum_a + ra[h, i].astype(F32)
        ta[h] = sum_a.astype(BF)
        last_a = [
            send(ta.at[h, up(x, k, NX)], ra2.at[h, i], at(xx=up(x, k, NX)))
            for i, k in enumerate(FAR4)
        ]
        yield
        res_a = tok[rows, :CA].astype(F32) + ta[h, x].astype(F32)
        res_b = tok[rows, CA:].astype(F32) + tb[h, y].astype(F32)
        for i, copy in reversed(list(enumerate(last_a))):
            arrive([copy])
            res_a = res_a + ra2[h, i].astype(F32)
        for i, copy in reversed(list(enumerate(last_b))):
            arrive([copy])
            res_b = res_b + rb2[h, i].astype(F32)
        res[h, :, :CA] = res_a.astype(BF)
        res[h, :, CA:] = res_b.astype(BF)

        yield from gather_hv(
            res.at[h, :, pl.ds(0, CA)], res.at[h, :, pl.ds(CA, CB)], ya.at[h], yb.at[h]
        )
        done = []
        yield from scatter_dm(
            lambda cc: logit_part(cc, h), p3.at[h], s3.at[h], r3.at[h], s4.at[h], r4.at[h], done
        )

        total = done[0]
        lane = lax.broadcasted_iota(jnp.int32, (OWN, VPAD), 1)
        ss = jnp.sum(
            jnp.where((lane == VOC) | (lane == VOC + 1), total, 0.0), axis=1, keepdims=True
        )
        logits = total * lax.rsqrt(ss / D + 1e-05)
        inside = lane < VOC
        top = jnp.max(jnp.where(inside, logits, LOW), axis=1, keepdims=True)
        mass = jnp.sum(jnp.where(inside, jnp.exp(logits - top), 0.0), axis=1, keepdims=True)
        row = lax.broadcasted_iota(jnp.int32, (OWN, 128), 0)
        col = lax.broadcasted_iota(jnp.int32, (OWN, 128), 1)
        spot = row // RH * ROWS + h * RH + lax.rem(row, RH)
        diag = col == spot + lax.rem(dm, 4) * (2 * ROWS)
        ids = gold[pl.ds(dm // 4, 1), :].astype(F32)
        wanted = jnp.sum(jnp.where(diag, ids, 0.0), axis=1, keepdims=True).astype(jnp.int32)
        hit = inside & (lane + hv * VOC == wanted)
        found = jnp.sum(jnp.where(hit, logits, 0.0), axis=1, keepdims=True)

        def flat(v, other):
            return jnp.where(diag, v, other)

        result.append(
            (
                jnp.max(flat(top, LOW), axis=0, keepdims=True),
                jnp.sum(flat(mass, 0.0), axis=0, keepdims=True),
                jnp.sum(flat(found, 0.0), axis=0, keepdims=True),
            )
        )

    def fold():
        g = gain[...]
        step = 32
        loads[3].wait()

        def some(i, carry):
            rows = pl.ds(pl.multiple_of(i * step, step), step)
            w_un[rows, :] = (w_raw[rows, :].astype(F32) * g).astype(BF)
            return carry

        whole = VOC // step
        lax.fori_loop(0, whole, some, 0)
        w_un[whole * step :, :] = jnp.zeros((VPAD - whole * step, WIDE), BF)
        w_un[whole * step : VOC, :] = (w_raw[whole * step :, :].astype(F32) * g).astype(BF)

    results = []
    active = [half(h, results) for h in range(NH)]
    turn = 0
    while active:
        for walk in list(active):
            if next(walk, active) is active:
                active.remove(walk)
        if turn == 0:
            fold()
        turn += 1

    def pack(t, m, f):
        line = lax.broadcasted_iota(jnp.int32, (8, 128), 0)
        return jnp.where(line == 0, t, jnp.where(line == 1, m, jnp.where(line == 2, f, 0.0)))

    def combine(tiles):
        best = tiles[0][0:1]
        for t in tiles[1:]:
            best = jnp.maximum(best, t[0:1])
        m = jnp.zeros((1, 128), F32)
        f = jnp.zeros((1, 128), F32)
        for t in tiles:
            m = m + t[1:2] * jnp.exp(t[0:1] - best)
            f = f + t[2:3]
        return best, m, f

    best, m, f = results[0]
    for t in results[1:]:
        best, m, f = jnp.maximum(best, t[0]), m + t[1], f + t[2]
    st1[0] = pack(best, m, f)
    copies = [send(st1.at[0], st1.at[1], at(cc=oc))]
    for i, k in enumerate(FAR4):
        copies.append(send(st1.at[0], st1.at[2 + 2 * i], at(xx=up(x, k, NX))))
        copies.append(send(st1.at[0], st1.at[3 + 2 * i], at(cc=oc, xx=up(x, k, NX))))
    arrive(copies)
    st2[0] = pack(*combine([st1[i] for i in range(8)]))
    copies = [
        send(st2.at[0], st2.at[1 + i], at(yy=up(y, k, NY))) for i, k in enumerate(FAR8)
    ]
    amount = lens[...].astype(F32)
    one = lax.broadcasted_iota(jnp.int32, (NOPT, NOPT), 0)
    two = lax.broadcasted_iota(jnp.int32, (NOPT, NOPT), 1)
    ends = jnp.sum(jnp.where(two <= one, amount, 0.0), axis=1, keepdims=True)
    length = jnp.sum(jnp.where(two == one, amount, 0.0), axis=1, keepdims=True)
    starts = ends - length
    arrive(copies)
    best, m, f = combine([st2[i] for i in range(8)])
    spot = lax.broadcasted_iota(jnp.int32, (1, 128), 1)
    base = lax.rem(z, 2) * (4 * ROWS)
    valid = (spot >= base) & (spot < base + 4 * ROWS)
    value = jnp.where(valid, f - best - jnp.log(jnp.where(valid, m, 1.0)), 0.0)
    st3[z] = jnp.broadcast_to(value, (8, 128))
    copies = [send(st3.at[z], st3.at[z], at(zz=up(z, k, NZ))) for k in FAR8]
    arrive(copies)
    col = lax.broadcasted_iota(jnp.int32, (NOPT, 128), 1)
    acc = jnp.zeros((NOPT, 1), F32)
    for i in range(4):
        line = st3[2 * i][0:1] + st3[2 * i + 1][0:1]
        lp_out[i : i + 1, :] = line
        where = (col + 128 * i).astype(F32)
        member = (where >= starts) & (where < ends)
        acc = acc + jnp.sum(jnp.where(member, line, 0.0), axis=1, keepdims=True)
    score = acc / length
    score_out[...] = jnp.sum(jnp.where(two == one, score, 0.0), axis=0, keepdims=True)
    sent()


def per_device(
    tokens, gate_weight, up_weight, down_weight, norm_gain, unembed, gold_ids, option_lengths
):
    vm = pl.BlockSpec(memory_space=pltpu.VMEM)
    anyspace = pl.BlockSpec(memory_space=pl.ANY)
    scratch = [
        pltpu.VMEM((2 * FF, WIDE), BF),
        pltpu.VMEM((FF, WIDE), BF),
        pltpu.VMEM((VOC, WIDE), BF),
        pltpu.VMEM((VPAD, WIDE), BF),
        pltpu.VMEM((NH, NY, NX, RH, CA), BF),
        pltpu.VMEM((NH, NY, NX, RH, CB), BF),
        pltpu.VMEM((NH, NZ, OWN, 2 * FF), BF),
        pltpu.VMEM((NH, NZ, OWN, 2 * FF), BF),
        pltpu.VMEM((NH, NZ, OWN, 2 * FF), F32),
        pltpu.VMEM((NH, NZ, OWN, 2 * FF), BF),
        pltpu.VMEM((NH, NZ - 1, OWN, 2 * FF), BF),
        pltpu.VMEM((NH, NZ, NC, OWN, FF), BF),
        pltpu.VMEM((NH, NY, NX, RH, CA), BF),
        pltpu.VMEM((NH, NY, NX, RH, CB), BF),
        pltpu.VMEM((NH, NY - 1, NX, RH, CA), BF),
        pltpu.VMEM((NH, NX - 1, NY, RH, CB), BF),
        pltpu.VMEM((NH, NX, RH, CA), BF),
        pltpu.VMEM((NH, NY, RH, CB), BF),
        pltpu.VMEM((NH, NX - 1, RH, CA), BF),
        pltpu.VMEM((NH, NY - 1, RH, CB), BF),
        pltpu.VMEM((NH, RH, WIDE), BF),
        pltpu.VMEM((NH, NY, NX, RH, CA), BF),
        pltpu.VMEM((NH, NY, NX, RH, CB), BF),
        pltpu.VMEM((NH, NZ, OWN, VPAD), BF),
        pltpu.VMEM((NH, NZ, OWN, VPAD), BF),
        pltpu.VMEM((NH, NZ, OWN, VPAD), F32),
        pltpu.VMEM((NH, NZ, OWN, VPAD), BF),
        pltpu.VMEM((NH, NZ - 1, OWN, VPAD), BF),
        pltpu.VMEM((8, 8, 128), F32),
        pltpu.VMEM((8, 8, 128), F32),
        pltpu.VMEM((8, 8, 128), F32),
        pltpu.SemaphoreType.DMA((COPIES,)),
        pltpu.SemaphoreType.DMA((COPIES,)),
        pltpu.SemaphoreType.DMA((4,)),
    ]
    logprob, score = pl.pallas_call(
        kernel,
        out_shape=(
            jax.ShapeDtypeStruct((4, 128), F32),
            jax.ShapeDtypeStruct((1, NOPT), F32),
        ),
        in_specs=[vm, anyspace, anyspace, anyspace, vm, anyspace, vm, vm],
        out_specs=(vm, vm),
        scratch_shapes=scratch,
        name="score",
        compiler_params=pltpu.CompilerParams(
            collective_id=0, has_side_effects=True, vmem_limit_bytes=56 << 20
        ),
    )(
        tokens,
        gate_weight.T,
        up_weight.T,
        down_weight,
        norm_gain.reshape(1, WIDE),
        unembed.T,
        gold_ids.reshape(4, 128),
        option_lengths.reshape(1, NOPT),
    )
    return logprob.reshape(512), score.reshape(NOPT)


def solution(mesh):
    placed = (
        P("hv", "dm"),
        P("dm", "hv"),
        P("dm", "hv"),
        P("hv", "dm"),
        P("dm"),
        P("dm", "hv"),
        P(),
        P(),
    )
    return jax.shard_map(
        per_device, mesh=mesh, in_specs=placed, out_specs=(P(), P()), check_vma=False
    )
```

```python
import jax
import jax.numpy as jnp
from jax import lax
from jax.experimental import pallas as pl
from jax.experimental.pallas import tpu as pltpu
from jax.sharding import PartitionSpec as P

D = 16384
NZ, NC, NY, NX = 8, 2, 8, 4
ROWS = 16
WIDE = 1024
FF = 416
VOC = 1002
VPAD = 1024
CA = 384
CB = WIDE - CA
NH = 2
RH = ROWS // NH
OWN = 2 * RH
NOPT = 32
FAR8 = (4, 3, 5, 2, 6, 1, 7)
FAR4 = (2, 1, 3)
LOW = -1e30
COPIES = 240
GA, GB, SA, SB, SZ = False, False, False, False, True
MESH = pl.DeviceIdType.MESH
BF = jnp.bfloat16
F32 = jnp.float32
NT = (((1,), (1,)), ((), ()))


def kernel(
    tok, wg, wu, wd, gain, un, gold, lens, lp_out, score_out,
    w_in, w_gu, w_down, w_raw, w_un, w_lm, xa, xb, s1, r1, p1, s2, r2, hid,
    qa, qb, ra, rb, ta, tb, ra2, rb2, res, ya, yb,
    s3, r3, p3, s4, r4, st1, st3, send_sem, recv_sem, local_sem,
):
    dm = lax.axis_index("dm")
    hv = lax.axis_index("hv")
    z, c = dm // NC, lax.rem(dm, NC)
    y, x = hv // NX, lax.rem(hv, NX)
    oc = 1 - c

    def at(zz=None, cc=None, yy=None, xx=None):
        zz = z if zz is None else zz
        cc = c if cc is None else cc
        yy = y if yy is None else yy
        xx = x if xx is None else xx
        return (zz * NC + cc, yy * NX + xx)

    def up(v, k, n):
        return lax.rem(v + k, n)

    loads = [
        pltpu.make_async_copy(wg, w_in.at[pl.ds(0, FF)], local_sem.at[0]),
        pltpu.make_async_copy(wu, w_in.at[pl.ds(FF, FF)], local_sem.at[1]),
        pltpu.make_async_copy(wd, w_down, local_sem.at[2]),
        pltpu.make_async_copy(un, w_raw, local_sem.at[3]),
    ]
    for load in loads:
        load.start()

    barrier = pltpu.get_barrier_semaphore()
    greet = (
        [at(yy=up(y, k, NY)) for k in FAR8]
        + [at(zz=up(z, k, NZ)) for k in FAR8]
        + [at(xx=up(x, k, NX)) for k in FAR4]
        + [at(cc=oc)]
    )
    for peer in greet:
        pl.semaphore_signal(barrier, inc=1, device_id=peer, device_id_type=MESH)
    pl.semaphore_wait(barrier, len(greet))

    count = [0]
    pending = []

    def send(src, dst, peer):
        n = count[0]
        count[0] = n + 1
        copy = pltpu.make_async_remote_copy(
            src_ref=src,
            dst_ref=dst,
            send_sem=send_sem.at[n],
            recv_sem=recv_sem.at[n],
            device_id=peer,
            device_id_type=MESH,
        )
        copy.start()
        pending.append(copy)
        return copy

    def sent():
        for copy in pending:
            copy.wait_send()
        pending.clear()

    def arrive(copies):
        for copy in copies:
            copy.wait_recv()

    def cut(n):
        return n // 256 * 128

    def left(ref):
        most = (slice(None),) * (len(ref.shape) - 1)
        return ref.at[most + (pl.ds(0, cut(ref.shape[-1])),)]

    def right(ref):
        n = ref.shape[-1]
        most = (slice(None),) * (len(ref.shape) - 1)
        return ref.at[most + (pl.ds(cut(n), n - cut(n)),)]

    def spread_start(src, slot, p, peer, relay):
        return [send(src, slot(p), peer(k)) for k in ((2, 6, 1, 7) if relay else FAR8)]

    def spread_relay(first, slot, p, peer, relay):
        if not relay:
            return first
        arrive(first[:1])
        near = slot(up(p, 6, 8))
        more = [send(left(near), left(near), peer(2)), send(near, near, peer(1))]
        arrive(first[1:2])
        near = slot(up(p, 2, 8))
        more += [send(right(near), right(near), peer(6)), send(near, near, peer(7))]
        return first[2:] + more

    def sum_start(out, p, peer, got, relay):
        if not relay:
            return [send(out.at[up(p, k, 8)], got.at[i], peer(k)) for i, k in enumerate(FAR8)]
        far = out.at[up(p, 4, 8)]
        return [
            send(left(far), left(got.at[2]), peer(2)),
            send(right(far), right(got.at[2]), peer(6)),
            send(out.at[up(p, 3, 8)], got.at[0], peer(1)),
            send(out.at[up(p, 5, 8)], got.at[1], peer(7)),
            send(out.at[up(p, 1, 8)], got.at[5], peer(1)),
            send(out.at[up(p, 7, 8)], got.at[6], peer(7)),
        ]

    def sum_relay(first, out, p, peer, got, relay):
        if not relay:
            return first
        k = cut(out.shape[-1])
        arrive(first[:1] + first[2:3])
        term = out[up(p, 2, 8)].astype(F32) + got[0].astype(F32)
        got[3, ..., :k] = (term[..., :k] + got[2, ..., :k].astype(F32)).astype(BF)
        got[3, ..., k:] = term[..., k:].astype(BF)
        more = [send(got.at[3], got.at[7], peer(2))]
        arrive(first[1:2] + first[3:4])
        term = out[up(p, 6, 8)].astype(F32) + got[1].astype(F32)
        got[4, ..., k:] = (term[..., k:] + got[2, ..., k:].astype(F32)).astype(BF)
        got[4, ..., :k] = term[..., :k].astype(BF)
        more += [send(got.at[4], got.at[8], peer(6))]
        return first[4:] + more

    def sum_end(last, total, got, relay):
        spots = (5, 6, 7, 8) if relay else tuple(range(7))
        order = list(zip(spots, last))
        for i, copy in order if relay else reversed(order):
            arrive([copy])
            total = total + got[i].astype(F32)
        return total

    def along_y(k):
        return at(yy=up(y, k, NY))

    def along_z(k):
        return at(zz=up(z, k, NZ))

    def gather_hv(block_a, block_b, ga, gb):
        def slot_a(i):
            return ga.at[i]

        def slot_b(i):
            return gb.at[i, x]

        first_a = [send(block_a, ga.at[y, x], at(xx=up(x, k, NX))) for k in FAR4]
        first_b = spread_start(block_b, slot_b, y, along_y, GB)
        ga[y, x] = block_a[...]
        gb[y, x] = block_b[...]
        yield
        arrive(first_a)
        last = spread_start(ga.at[y], slot_a, y, along_y, GA)
        arrive(spread_relay(first_b, slot_b, y, along_y, GB))
        more = [send(gb.at[:, x], gb.at[:, x], at(xx=up(x, k, NX))) for k in FAR4]
        last = spread_relay(last, slot_a, y, along_y, GA)
        yield
        arrive(last + more)

    def part(ga, gb, cc):
        n = NY * 2 * RH
        a = ga[:, pl.ds(2 * cc, 2)].reshape(n, CA)
        b = gb[:, pl.ds(2 * cc, 2)].reshape(n, CB)
        return a, b

    def product(a, b, w):
        return jnp.dot(a, w[:CA, :], preferred_element_type=F32) + jnp.dot(
            b, w[CA:, :], preferred_element_type=F32
        )

    def scatter_dm(make, mine, out, got, out2, got2, done):
        out[...] = make(oc).astype(BF)
        swap = send(out, got, at(cc=oc))
        mine[...] = make(c)
        arrive([swap])
        out2[...] = (mine[...] + got[...].astype(F32)).astype(BF)
        copies = sum_start(out2, z, along_z, got2, SZ)
        total = mine[z] + got[z].astype(F32)
        yield
        copies = sum_relay(copies, out2, z, along_z, got2, SZ)
        if SZ:
            yield
        done.append(sum_end(copies, total, got2, SZ))

    def gate_up(cc, h):
        a, b = part(xa.at[h], xb.at[h], cc)
        return product(a, b, w_gu[...]).reshape(NZ, OWN, 2 * FF)

    def logit_part(cc, h):
        a, b = part(ya.at[h], yb.at[h], cc)
        out = product(a, b, w_lm[...])
        wide_a, wide_b = a.astype(F32), b.astype(F32)
        ss = jnp.sum(wide_a * wide_a, axis=1, keepdims=True) + jnp.sum(
            wide_b * wide_b, axis=1, keepdims=True
        )
        high = ss.astype(BF).astype(F32)
        tail = out[:, VPAD - 128 :]
        lane = lax.broadcasted_iota(jnp.int32, tail.shape, 1) + (VPAD - 128)
        tail = jnp.where(lane == VOC, high, jnp.where(lane == VOC + 1, ss - high, tail))
        out = jnp.concatenate([out[:, : VPAD - 128], tail], axis=1)
        return out.reshape(NZ, OWN, VPAD)

    def half(h, result):
        rows = pl.ds(h * RH, RH)
        yield from gather_hv(
            tok.at[rows, pl.ds(0, CA)], tok.at[rows, pl.ds(CA, CB)], xa.at[h], xb.at[h]
        )
        done = []
        yield from scatter_dm(
            lambda cc: gate_up(cc, h), p1.at[h], s1.at[h], r1.at[h], s2.at[h], r2.at[h], done
        )
        gate, upper = done[0][:, :FF], done[0][:, FF:]
        mine = hid.at[h]
        mine[z, c] = (gate / (1.0 + jnp.exp(-gate)) * upper).astype(BF)

        far = [send(mine.at[z, c], mine.at[z, c], at(zz=up(z, k, NZ))) for k in FAR8]
        near = [send(mine.at[z, c], mine.at[z, c], at(cc=oc))]
        yield
        for k, copy in reversed(list(zip(FAR8, far))):
            arrive([copy])
            origin = up(z, NZ - k, NZ)
            near.append(send(mine.at[origin, c], mine.at[origin, c], at(cc=oc)))
        arrive(near)

        q = jnp.dot(
            mine[...].reshape(NZ * NC * OWN, FF), w_down[...], preferred_element_type=F32
        )
        q = q.reshape(NY, NX, RH, WIDE).astype(BF)
        qa[h] = q[..., :CA]
        first_a = sum_start(qa.at[h], y, along_y, ra.at[h], SA)
        qb[h] = q[..., CA:]
        first_b = [
            send(qb.at[h, :, up(x, k, NX)], rb.at[h, i], at(xx=up(x, k, NX)))
            for i, k in enumerate(FAR4)
        ]
        yield
        first_a = sum_relay(first_a, qa.at[h], y, along_y, ra.at[h], SA)
        sum_b = qb[h, :, x].astype(F32)
        for i, copy in reversed(list(enumerate(first_b))):
            arrive([copy])
            sum_b = sum_b + rb[h, i].astype(F32)
        tb[h] = sum_b.astype(BF)
        last_b = sum_start(tb.at[h], y, along_y, rb2.at[h], SB)
        ta[h] = sum_end(first_a, qa[h, y].astype(F32), ra.at[h], SA).astype(BF)
        last_a = [
            send(ta.at[h, up(x, k, NX)], ra2.at[h, i], at(xx=up(x, k, NX)))
            for i, k in enumerate(FAR4)
        ]
        yield
        last_b = sum_relay(last_b, tb.at[h], y, along_y, rb2.at[h], SB)
        res_a = tok[rows, :CA].astype(F32) + ta[h, x].astype(F32)
        res_b = tok[rows, CA:].astype(F32) + tb[h, y].astype(F32)
        for i, copy in reversed(list(enumerate(last_a))):
            arrive([copy])
            res_a = res_a + ra2[h, i].astype(F32)
        res_b = sum_end(last_b, res_b, rb2.at[h], SB)
        res[h, :, :CA] = res_a.astype(BF)
        res[h, :, CA:] = res_b.astype(BF)

        yield from gather_hv(
            res.at[h, :, pl.ds(0, CA)], res.at[h, :, pl.ds(CA, CB)], ya.at[h], yb.at[h]
        )
        done = []
        yield from scatter_dm(
            lambda cc: logit_part(cc, h), p3.at[h], s3.at[h], r3.at[h], s4.at[h], r4.at[h], done
        )

        total = done[0]
        lane = lax.broadcasted_iota(jnp.int32, (OWN, VPAD), 1)
        ss = jnp.sum(
            jnp.where((lane == VOC) | (lane == VOC + 1), total, 0.0), axis=1, keepdims=True
        )
        logits = total * lax.rsqrt(ss / D + 1e-05)
        inside = lane < VOC
        top = jnp.max(jnp.where(inside, logits, LOW), axis=1, keepdims=True)
        mass = jnp.sum(jnp.where(inside, jnp.exp(logits - top), 0.0), axis=1, keepdims=True)
        row = lax.broadcasted_iota(jnp.int32, (OWN, 128), 0)
        col = lax.broadcasted_iota(jnp.int32, (OWN, 128), 1)
        spot = row // RH * ROWS + h * RH + lax.rem(row, RH) + lax.rem(dm, 4) * (2 * ROWS)
        diag = col == spot
        ids = gold[pl.ds(dm // 4, 1), :].astype(F32)
        wanted = jnp.sum(jnp.where(diag, ids, 0.0), axis=1, keepdims=True).astype(jnp.int32)
        hit = inside & (lane + hv * VOC == wanted)
        found = jnp.sum(jnp.where(hit, logits, 0.0), axis=1, keepdims=True)

        level = top + jnp.log(mass)
        other = col == lax.rem(spot + 2 * ROWS, 128)
        line = jnp.where(diag, level, jnp.where(other, found, 0.0))
        result.append(jnp.sum(line, axis=0, keepdims=True))

    def fold():
        g = gain[...]
        step = 32
        for load in loads:
            load.wait()
        w_gu[...] = w_in[...].T

        def some(i, carry):
            rows = pl.ds(pl.multiple_of(i * step, step), step)
            w_un[rows, :] = (w_raw[rows, :].astype(F32) * g).astype(BF)
            return carry

        whole = VOC // step
        lax.fori_loop(0, whole, some, 0)
        w_un[whole * step :, :] = jnp.zeros((VPAD - whole * step, WIDE), BF)
        w_un[whole * step : VOC, :] = (w_raw[whole * step :, :].astype(F32) * g).astype(BF)
        w_lm[...] = w_un[...].T

    results = []
    active = [half(h, results) for h in range(NH)]
    turn = 0
    while active:
        for walk in list(active):
            if next(walk, active) is active:
                active.remove(walk)
        if turn == 0:
            fold()
        turn += 1

    line = results[0]
    for t in results[1:]:
        line = line + t
    st1[hv] = line
    copies = [
        send(st1.at[hv], st1.at[hv], at(yy=up(y, j, NY), xx=up(x, k, NX)))
        for j in (4, 3, 5, 2, 6, 1, 7, 0)
        for k in (2, 1, 3, 0)
        if j or k
    ]
    amount = lens[...].astype(F32)
    one = lax.broadcasted_iota(jnp.int32, (NOPT, NOPT), 0)
    two = lax.broadcasted_iota(jnp.int32, (NOPT, NOPT), 1)
    ends = jnp.sum(jnp.where(two <= one, amount, 0.0), axis=1, keepdims=True)
    length = jnp.sum(jnp.where(two == one, amount, 0.0), axis=1, keepdims=True)
    starts = ends - length
    arrive(copies)
    lines = [st1[i] for i in range(NY * NX)]
    best = lines[0]
    for t in lines[1:]:
        best = jnp.maximum(best, t)
    mass = jnp.zeros((1, 128), F32)
    found = jnp.zeros((1, 128), F32)
    for t in lines:
        mass = mass + jnp.exp(t - best)
        found = found + t
    level = best + jnp.log(mass)
    spot = lax.broadcasted_iota(jnp.int32, (1, 128), 1)
    base = lax.rem(dm, 4) * (2 * ROWS)
    valid = (spot >= base) & (spot < base + 2 * ROWS)
    st3[dm] = jnp.where(valid, pltpu.roll(found, 128 - 2 * ROWS, 1) - level, 0.0)
    copies = [
        send(st3.at[dm], st3.at[dm], at(zz=up(z, k, NZ), cc=up(c, e, NC)))
        for k in (4, 3, 5, 2, 6, 1, 7, 0)
        for e in (0, 1)
        if k or e
    ]
    arrive(copies)
    col = lax.broadcasted_iota(jnp.int32, (NOPT, 128), 1)
    acc = jnp.zeros((NOPT, 1), F32)
    for i in range(4):
        line = st3[4 * i] + st3[4 * i + 1] + st3[4 * i + 2] + st3[4 * i + 3]
        lp_out[i : i + 1, :] = line
        where = (col + 128 * i).astype(F32)
        member = (where >= starts) & (where < ends)
        acc = acc + jnp.sum(jnp.where(member, line, 0.0), axis=1, keepdims=True)
    score = acc / length
    score_out[...] = jnp.sum(jnp.where(two == one, score, 0.0), axis=0, keepdims=True)
    sent()


def per_device(
    tokens, gate_weight, up_weight, down_weight, norm_gain, unembed, gold_ids, option_lengths
):
    vm = pl.BlockSpec(memory_space=pltpu.VMEM)
    anyspace = pl.BlockSpec(memory_space=pl.ANY)
    scratch = [
        pltpu.VMEM((2 * FF, WIDE), BF),
        pltpu.VMEM((WIDE, 2 * FF), BF),
        pltpu.VMEM((FF, WIDE), BF),
        pltpu.VMEM((VOC, WIDE), BF),
        pltpu.VMEM((VPAD, WIDE), BF),
        pltpu.VMEM((WIDE, VPAD), BF),
        pltpu.VMEM((NH, NY, NX, RH, CA), BF),
        pltpu.VMEM((NH, NY, NX, RH, CB), BF),
        pltpu.VMEM((NH, NZ, OWN, 2 * FF), BF),
        pltpu.VMEM((NH, NZ, OWN, 2 * FF), BF),
        pltpu.VMEM((NH, NZ, OWN, 2 * FF), F32),
        pltpu.VMEM((NH, NZ, OWN, 2 * FF), BF),
        pltpu.VMEM((NH, 9, OWN, 2 * FF), BF),
        pltpu.VMEM((NH, NZ, NC, OWN, FF), BF),
        pltpu.VMEM((NH, NY, NX, RH, CA), BF),
        pltpu.VMEM((NH, NY, NX, RH, CB), BF),
        pltpu.VMEM((NH, 9, NX, RH, CA), BF),
        pltpu.VMEM((NH, NX - 1, NY, RH, CB), BF),
        pltpu.VMEM((NH, NX, RH, CA), BF),
        pltpu.VMEM((NH, NY, RH, CB), BF),
        pltpu.VMEM((NH, NX - 1, RH, CA), BF),
        pltpu.VMEM((NH, 9, RH, CB), BF),
        pltpu.VMEM((NH, RH, WIDE), BF),
        pltpu.VMEM((NH, NY, NX, RH, CA), BF),
        pltpu.VMEM((NH, NY, NX, RH, CB), BF),
        pltpu.VMEM((NH, NZ, OWN, VPAD), BF),
        pltpu.VMEM((NH, NZ, OWN, VPAD), BF),
        pltpu.VMEM((NH, NZ, OWN, VPAD), F32),
        pltpu.VMEM((NH, NZ, OWN, VPAD), BF),
        pltpu.VMEM((NH, 9, OWN, VPAD), BF),
        pltpu.VMEM((NY * NX, 1, 128), F32),
        pltpu.VMEM((NZ * NC, 1, 128), F32),
        pltpu.SemaphoreType.DMA((COPIES,)),
        pltpu.SemaphoreType.DMA((COPIES,)),
        pltpu.SemaphoreType.DMA((4,)),
    ]
    logprob, score = pl.pallas_call(
        kernel,
        out_shape=(
            jax.ShapeDtypeStruct((4, 128), F32),
            jax.ShapeDtypeStruct((1, NOPT), F32),
        ),
        in_specs=[vm, anyspace, anyspace, anyspace, vm, anyspace, vm, vm],
        out_specs=(vm, vm),
        scratch_shapes=scratch,
        name="score",
        compiler_params=pltpu.CompilerParams(
            collective_id=0, has_side_effects=True, vmem_limit_bytes=56 << 20
        ),
    )(
        tokens,
        gate_weight.T,
        up_weight.T,
        down_weight,
        norm_gain.reshape(1, WIDE),
        unembed.T,
        gold_ids.reshape(4, 128),
        option_lengths.reshape(1, NOPT),
    )
    return logprob.reshape(512), score.reshape(NOPT)


def solution(mesh):
    placed = (
        P("hv", "dm"),
        P("dm", "hv"),
        P("dm", "hv"),
        P("hv", "dm"),
        P("dm"),
        P("dm", "hv"),
        P(),
        P(),
    )
    return jax.shard_map(
        per_device, mesh=mesh, in_specs=placed, out_specs=(P(), P()), check_vma=False
    )
```

```python
import jax
import jax.numpy as jnp
from jax import lax
from jax.experimental import pallas as pl
from jax.experimental.pallas import tpu as pltpu
from jax.sharding import PartitionSpec as P

D = 16384
NZ, NC, NY, NX = 8, 2, 8, 4
ROWS = 16
WIDE = 1024
FF = 416
VOC = 1002
VPAD = 1024
CA = 384
CB = WIDE - CA
NH = 2
RH = ROWS // NH
OWN = 2 * RH
NOPT = 32
FAR8 = (4, 3, 5, 2, 6, 1, 7)
FAR4 = (2, 1, 3)
LOW = -1e30
COPIES = 240
GA, GB, SA, SB, SZ = False, False, False, False, True
MESH = pl.DeviceIdType.MESH
BF = jnp.bfloat16
F32 = jnp.float32
NT = (((1,), (1,)), ((), ()))


def kernel(
    tok, wg, wu, wd, gain, un, gold, lp_out,
    w_in, w_gu, w_down, w_raw, w_un, w_lm, xa, xb, s1, r1, p1, s2, r2, hid,
    qa, qb, ra, rb, ta, tb, ra2, rb2, res, ya, yb,
    s3, r3, p3, s4, r4, st1, st3, send_sem, recv_sem, local_sem,
):
    dm = lax.axis_index("dm")
    hv = lax.axis_index("hv")
    z, c = dm // NC, lax.rem(dm, NC)
    y, x = hv // NX, lax.rem(hv, NX)
    oc = 1 - c

    def at(zz=None, cc=None, yy=None, xx=None):
        zz = z if zz is None else zz
        cc = c if cc is None else cc
        yy = y if yy is None else yy
        xx = x if xx is None else xx
        return (zz * NC + cc, yy * NX + xx)

    def up(v, k, n):
        return lax.rem(v + k, n)

    loads = [
        pltpu.make_async_copy(wg, w_in.at[pl.ds(0, FF)], local_sem.at[0]),
        pltpu.make_async_copy(wu, w_in.at[pl.ds(FF, FF)], local_sem.at[1]),
        pltpu.make_async_copy(wd, w_down, local_sem.at[2]),
        pltpu.make_async_copy(un, w_raw, local_sem.at[3]),
    ]
    for load in loads:
        load.start()

    barrier = pltpu.get_barrier_semaphore()
    greet = (
        [at(yy=up(y, k, NY)) for k in FAR8]
        + [at(zz=up(z, k, NZ)) for k in FAR8]
        + [at(xx=up(x, k, NX)) for k in FAR4]
        + [at(cc=oc)]
    )
    for peer in greet:
        pl.semaphore_signal(barrier, inc=1, device_id=peer, device_id_type=MESH)
    pl.semaphore_wait(barrier, len(greet))

    count = [0]
    pending = []

    def send(src, dst, peer):
        n = count[0]
        count[0] = n + 1
        copy = pltpu.make_async_remote_copy(
            src_ref=src,
            dst_ref=dst,
            send_sem=send_sem.at[n],
            recv_sem=recv_sem.at[n],
            device_id=peer,
            device_id_type=MESH,
        )
        copy.start()
        pending.append(copy)
        return copy

    def sent(keep=0):
        done = pending[: len(pending) - keep]
        for copy in done:
            copy.wait_send()
        del pending[: len(done)]

    def arrive(copies):
        for copy in copies:
            copy.wait_recv()

    def cut(n):
        return n // 256 * 128

    def left(ref):
        most = (slice(None),) * (len(ref.shape) - 1)
        return ref.at[most + (pl.ds(0, cut(ref.shape[-1])),)]

    def right(ref):
        n = ref.shape[-1]
        most = (slice(None),) * (len(ref.shape) - 1)
        return ref.at[most + (pl.ds(cut(n), n - cut(n)),)]

    def spread_start(src, slot, p, peer, relay):
        return [send(src, slot(p), peer(k)) for k in ((2, 6, 1, 7) if relay else FAR8)]

    def spread_relay(first, slot, p, peer, relay):
        if not relay:
            return first
        arrive(first[:1])
        near = slot(up(p, 6, 8))
        more = [send(left(near), left(near), peer(2)), send(near, near, peer(1))]
        arrive(first[1:2])
        near = slot(up(p, 2, 8))
        more += [send(right(near), right(near), peer(6)), send(near, near, peer(7))]
        return first[2:] + more

    def sum_start(out, p, peer, got, relay):
        if not relay:
            return [send(out.at[up(p, k, 8)], got.at[i], peer(k)) for i, k in enumerate(FAR8)]
        far = out.at[up(p, 4, 8)]
        return [
            send(left(far), left(got.at[2]), peer(2)),
            send(right(far), right(got.at[2]), peer(6)),
            send(out.at[up(p, 3, 8)], got.at[0], peer(1)),
            send(out.at[up(p, 5, 8)], got.at[1], peer(7)),
            send(out.at[up(p, 1, 8)], got.at[5], peer(1)),
            send(out.at[up(p, 7, 8)], got.at[6], peer(7)),
        ]

    def sum_relay(first, out, p, peer, got, relay):
        if not relay:
            return first
        k = cut(out.shape[-1])
        arrive(first[:1] + first[2:3])
        term = out[up(p, 2, 8)].astype(F32) + got[0].astype(F32)
        got[3, ..., :k] = (term[..., :k] + got[2, ..., :k].astype(F32)).astype(BF)
        got[3, ..., k:] = term[..., k:].astype(BF)
        more = [send(got.at[3], got.at[7], peer(2))]
        arrive(first[1:2] + first[3:4])
        term = out[up(p, 6, 8)].astype(F32) + got[1].astype(F32)
        got[4, ..., k:] = (term[..., k:] + got[2, ..., k:].astype(F32)).astype(BF)
        got[4, ..., :k] = term[..., :k].astype(BF)
        more += [send(got.at[4], got.at[8], peer(6))]
        return first[4:] + more

    def sum_end(last, total, got, relay):
        spots = (5, 6, 7, 8) if relay else tuple(range(7))
        order = list(zip(spots, last))
        for i, copy in order if relay else reversed(order):
            arrive([copy])
            total = total + got[i].astype(F32)
        return total

    def along_y(k):
        return at(yy=up(y, k, NY))

    def along_z(k):
        return at(zz=up(z, k, NZ))

    def gather_hv(block_a, block_b, ga, gb):
        def slot_a(i):
            return ga.at[i]

        def slot_b(i):
            return gb.at[i, x]

        first_a = [send(block_a, ga.at[y, x], at(xx=up(x, k, NX))) for k in FAR4]
        first_b = spread_start(block_b, slot_b, y, along_y, GB)
        ga[y, x] = block_a[...]
        gb[y, x] = block_b[...]
        yield
        arrive(first_a)
        last = spread_start(ga.at[y], slot_a, y, along_y, GA)
        arrive(spread_relay(first_b, slot_b, y, along_y, GB))
        more = [send(gb.at[:, x], gb.at[:, x], at(xx=up(x, k, NX))) for k in FAR4]
        last = spread_relay(last, slot_a, y, along_y, GA)
        yield
        arrive(last + more)

    def part(ga, gb, cc):
        n = NY * 2 * RH
        a = ga[:, pl.ds(2 * cc, 2)].reshape(n, CA)
        b = gb[:, pl.ds(2 * cc, 2)].reshape(n, CB)
        return a, b

    def product(a, b, w):
        return jnp.dot(a, w[:CA, :], preferred_element_type=F32) + jnp.dot(
            b, w[CA:, :], preferred_element_type=F32
        )

    def scatter_dm(make, mine, out, got, out2, got2, done):
        out[...] = make(oc).astype(BF)
        swap = send(out, got, at(cc=oc))
        mine[...] = make(c)
        arrive([swap])
        out2[...] = (mine[...] + got[...].astype(F32)).astype(BF)
        copies = sum_start(out2, z, along_z, got2, SZ)
        total = mine[z] + got[z].astype(F32)
        yield
        copies = sum_relay(copies, out2, z, along_z, got2, SZ)
        if SZ:
            yield
        done.append(sum_end(copies, total, got2, SZ))

    def gate_up(cc, h):
        a, b = part(xa.at[h], xb.at[h], cc)
        return product(a, b, w_gu[...]).reshape(NZ, OWN, 2 * FF)

    def logit_part(cc, h):
        a, b = part(ya.at[h], yb.at[h], cc)
        out = product(a, b, w_lm[...])
        wide_a, wide_b = a.astype(F32), b.astype(F32)
        ss = jnp.sum(wide_a * wide_a, axis=1, keepdims=True) + jnp.sum(
            wide_b * wide_b, axis=1, keepdims=True
        )
        high = ss.astype(BF).astype(F32)
        tail = out[:, VPAD - 128 :]
        lane = lax.broadcasted_iota(jnp.int32, tail.shape, 1) + (VPAD - 128)
        tail = jnp.where(lane == VOC, high, jnp.where(lane == VOC + 1, ss - high, tail))
        out = jnp.concatenate([out[:, : VPAD - 128], tail], axis=1)
        return out.reshape(NZ, OWN, VPAD)

    def half(h, result):
        rows = pl.ds(h * RH, RH)
        yield from gather_hv(
            tok.at[rows, pl.ds(0, CA)], tok.at[rows, pl.ds(CA, CB)], xa.at[h], xb.at[h]
        )
        done = []
        yield from scatter_dm(
            lambda cc: gate_up(cc, h), p1.at[h], s1.at[h], r1.at[h], s2.at[h], r2.at[h], done
        )
        gate, upper = done[0][:, :FF], done[0][:, FF:]
        mine = hid.at[h]
        mine[z, c] = (gate / (1.0 + jnp.exp(-gate)) * upper).astype(BF)

        far = [send(mine.at[z, c], mine.at[z, c], at(zz=up(z, k, NZ))) for k in FAR8]
        near = [send(mine.at[z, c], mine.at[z, c], at(cc=oc))]
        yield
        for k, copy in reversed(list(zip(FAR8, far))):
            arrive([copy])
            origin = up(z, NZ - k, NZ)
            near.append(send(mine.at[origin, c], mine.at[origin, c], at(cc=oc)))
        arrive(near)

        q = jnp.dot(
            mine[...].reshape(NZ * NC * OWN, FF), w_down[...], preferred_element_type=F32
        )
        q = q.reshape(NY, NX, RH, WIDE).astype(BF)
        qa[h] = q[..., :CA]
        first_a = sum_start(qa.at[h], y, along_y, ra.at[h], SA)
        qb[h] = q[..., CA:]
        first_b = [
            send(qb.at[h, :, up(x, k, NX)], rb.at[h, i], at(xx=up(x, k, NX)))
            for i, k in enumerate(FAR4)
        ]
        yield
        first_a = sum_relay(first_a, qa.at[h], y, along_y, ra.at[h], SA)
        sum_b = qb[h, :, x].astype(F32)
        for i, copy in reversed(list(enumerate(first_b))):
            arrive([copy])
            sum_b = sum_b + rb[h, i].astype(F32)
        tb[h] = sum_b.astype(BF)
        last_b = sum_start(tb.at[h], y, along_y, rb2.at[h], SB)
        ta[h] = sum_end(first_a, qa[h, y].astype(F32), ra.at[h], SA).astype(BF)
        last_a = [
            send(ta.at[h, up(x, k, NX)], ra2.at[h, i], at(xx=up(x, k, NX)))
            for i, k in enumerate(FAR4)
        ]
        yield
        last_b = sum_relay(last_b, tb.at[h], y, along_y, rb2.at[h], SB)
        res_a = tok[rows, :CA].astype(F32) + ta[h, x].astype(F32)
        res_b = tok[rows, CA:].astype(F32) + tb[h, y].astype(F32)
        for i, copy in reversed(list(enumerate(last_a))):
            arrive([copy])
            res_a = res_a + ra2[h, i].astype(F32)
        res_b = sum_end(last_b, res_b, rb2.at[h], SB)
        res[h, :, :CA] = res_a.astype(BF)
        res[h, :, CA:] = res_b.astype(BF)

        yield from gather_hv(
            res.at[h, :, pl.ds(0, CA)], res.at[h, :, pl.ds(CA, CB)], ya.at[h], yb.at[h]
        )
        done = []
        yield from scatter_dm(
            lambda cc: logit_part(cc, h), p3.at[h], s3.at[h], r3.at[h], s4.at[h], r4.at[h], done
        )

        total = done[0]
        lane = lax.broadcasted_iota(jnp.int32, (OWN, VPAD), 1)
        ss = jnp.sum(
            jnp.where((lane == VOC) | (lane == VOC + 1), total, 0.0), axis=1, keepdims=True
        )
        logits = total * lax.rsqrt(ss / D + 1e-05)
        inside = lane < VOC
        top = jnp.max(jnp.where(inside, logits, LOW), axis=1, keepdims=True)
        mass = jnp.sum(jnp.where(inside, jnp.exp(logits - top), 0.0), axis=1, keepdims=True)
        row = lax.broadcasted_iota(jnp.int32, (OWN, 128), 0)
        col = lax.broadcasted_iota(jnp.int32, (OWN, 128), 1)
        spot = row // RH * ROWS + h * RH + lax.rem(row, RH) + lax.rem(dm, 4) * (2 * ROWS)
        diag = col == spot
        ids = gold[pl.ds(dm // 4, 1), :].astype(F32)
        wanted = jnp.sum(jnp.where(diag, ids, 0.0), axis=1, keepdims=True).astype(jnp.int32)
        hit = inside & (lane + hv * VOC == wanted)
        found = jnp.sum(jnp.where(hit, logits, 0.0), axis=1, keepdims=True)

        level = top + jnp.log(mass)
        other = col == lax.rem(spot + 2 * ROWS, 128)
        line = jnp.where(diag, level, jnp.where(other, found, 0.0))
        result.append(jnp.sum(line, axis=0, keepdims=True))

    def fold():
        g = gain[...]
        step = 32
        for load in loads:
            load.wait()
        w_gu[...] = w_in[...].T

        def some(i, carry):
            rows = pl.ds(pl.multiple_of(i * step, step), step)
            w_un[rows, :] = (w_raw[rows, :].astype(F32) * g).astype(BF)
            return carry

        whole = VOC // step
        lax.fori_loop(0, whole, some, 0)
        w_un[whole * step :, :] = jnp.zeros((VPAD - whole * step, WIDE), BF)
        w_un[whole * step : VOC, :] = (w_raw[whole * step :, :].astype(F32) * g).astype(BF)
        w_lm[...] = w_un[...].T

    results = []
    active = [half(h, results) for h in range(NH)]
    turn = 0
    while active:
        for walk in list(active):
            if next(walk, active) is active:
                active.remove(walk)
        if turn == 0:
            fold()
        turn += 1

    line = results[0]
    for t in results[1:]:
        line = line + t
    st1[hv] = line
    copies = [
        send(st1.at[hv], st1.at[hv], at(yy=up(y, j, NY), xx=up(x, k, NX)))
        for j in (4, 3, 5, 2, 6, 1, 7, 0)
        for k in (2, 1, 3, 0)
        if j or k
    ]
    sent(len(copies))
    arrive(copies)
    lines = [st1[i] for i in range(NY * NX)]
    best = lines[0]
    for t in lines[1:]:
        best = jnp.maximum(best, t)
    mass = jnp.zeros((1, 128), F32)
    found = jnp.zeros((1, 128), F32)
    for t in lines:
        mass = mass + jnp.exp(t - best)
        found = found + t
    level = best + jnp.log(mass)
    spot = lax.broadcasted_iota(jnp.int32, (1, 128), 1)
    base = lax.rem(dm, 4) * (2 * ROWS)
    valid = (spot >= base) & (spot < base + 2 * ROWS)
    st3[dm] = jnp.where(valid, pltpu.roll(found, 128 - 2 * ROWS, 1) - level, 0.0)
    copies = [
        send(st3.at[dm], st3.at[dm], at(zz=up(z, k, NZ), cc=up(c, e, NC)))
        for k in (4, 3, 5, 2, 6, 1, 7, 0)
        for e in (0, 1)
        if k or e
    ]
    sent(len(copies))
    arrive(copies)
    for i in range(4):
        lp_out[i : i + 1, :] = st3[4 * i] + st3[4 * i + 1] + st3[4 * i + 2] + st3[4 * i + 3]
    sent()


def options(lp, lens, lp_out, score_out):
    amount = lens[...].astype(F32)
    one = lax.broadcasted_iota(jnp.int32, (NOPT, NOPT), 0)
    two = lax.broadcasted_iota(jnp.int32, (NOPT, NOPT), 1)
    ends = jnp.sum(jnp.where(two <= one, amount, 0.0), axis=1, keepdims=True)
    length = jnp.sum(jnp.where(two == one, amount, 0.0), axis=1, keepdims=True)
    starts = ends - length
    col = lax.broadcasted_iota(jnp.int32, (NOPT, 128), 1)
    acc = jnp.zeros((NOPT, 1), F32)
    lp_out[...] = lp[...]
    for i in range(4):
        where = (col + 128 * i).astype(F32)
        member = (where >= starts) & (where < ends)
        acc = acc + jnp.sum(jnp.where(member, lp[i : i + 1, :], 0.0), axis=1, keepdims=True)
    score = acc / length
    score_out[...] = jnp.sum(jnp.where(two == one, score, 0.0), axis=0, keepdims=True)


def per_device(
    tokens, gate_weight, up_weight, down_weight, norm_gain, unembed, gold_ids, option_lengths
):
    vm = pl.BlockSpec(memory_space=pltpu.VMEM)
    anyspace = pl.BlockSpec(memory_space=pl.ANY)
    scratch = [
        pltpu.VMEM((2 * FF, WIDE), BF),
        pltpu.VMEM((WIDE, 2 * FF), BF),
        pltpu.VMEM((FF, WIDE), BF),
        pltpu.VMEM((VOC, WIDE), BF),
        pltpu.VMEM((VPAD, WIDE), BF),
        pltpu.VMEM((WIDE, VPAD), BF),
        pltpu.VMEM((NH, NY, NX, RH, CA), BF),
        pltpu.VMEM((NH, NY, NX, RH, CB), BF),
        pltpu.VMEM((NH, NZ, OWN, 2 * FF), BF),
        pltpu.VMEM((NH, NZ, OWN, 2 * FF), BF),
        pltpu.VMEM((NH, NZ, OWN, 2 * FF), F32),
        pltpu.VMEM((NH, NZ, OWN, 2 * FF), BF),
        pltpu.VMEM((NH, 9, OWN, 2 * FF), BF),
        pltpu.VMEM((NH, NZ, NC, OWN, FF), BF),
        pltpu.VMEM((NH, NY, NX, RH, CA), BF),
        pltpu.VMEM((NH, NY, NX, RH, CB), BF),
        pltpu.VMEM((NH, 9, NX, RH, CA), BF),
        pltpu.VMEM((NH, NX - 1, NY, RH, CB), BF),
        pltpu.VMEM((NH, NX, RH, CA), BF),
        pltpu.VMEM((NH, NY, RH, CB), BF),
        pltpu.VMEM((NH, NX - 1, RH, CA), BF),
        pltpu.VMEM((NH, 9, RH, CB), BF),
        pltpu.VMEM((NH, RH, WIDE), BF),
        pltpu.VMEM((NH, NY, NX, RH, CA), BF),
        pltpu.VMEM((NH, NY, NX, RH, CB), BF),
        pltpu.VMEM((NH, NZ, OWN, VPAD), BF),
        pltpu.VMEM((NH, NZ, OWN, VPAD), BF),
        pltpu.VMEM((NH, NZ, OWN, VPAD), F32),
        pltpu.VMEM((NH, NZ, OWN, VPAD), BF),
        pltpu.VMEM((NH, 9, OWN, VPAD), BF),
        pltpu.VMEM((NY * NX, 1, 128), F32),
        pltpu.VMEM((NZ * NC, 1, 128), F32),
        pltpu.SemaphoreType.DMA((COPIES,)),
        pltpu.SemaphoreType.DMA((COPIES,)),
        pltpu.SemaphoreType.DMA((4,)),
    ]
    raw = pl.pallas_call(
        kernel,
        out_shape=jax.ShapeDtypeStruct((4, 128), F32),
        in_specs=[vm, anyspace, anyspace, anyspace, vm, anyspace, vm],
        out_specs=vm,
        scratch_shapes=scratch,
        name="score",
        compiler_params=pltpu.CompilerParams(
            collective_id=0, has_side_effects=True, vmem_limit_bytes=56 << 20
        ),
    )(
        tokens,
        gate_weight.T,
        up_weight.T,
        down_weight,
        norm_gain.reshape(1, WIDE),
        unembed.T,
        gold_ids.reshape(4, 128),
    )
    logprob, score = pl.pallas_call(
        options,
        out_shape=(
            jax.ShapeDtypeStruct((4, 128), F32),
            jax.ShapeDtypeStruct((1, NOPT), F32),
        ),
        in_specs=[vm, vm],
        out_specs=(vm, vm),
        name="options",
    )(raw, option_lengths.reshape(1, NOPT))
    return logprob.reshape(512), score.reshape(NOPT)


def solution(mesh):
    placed = (
        P("hv", "dm"),
        P("dm", "hv"),
        P("dm", "hv"),
        P("hv", "dm"),
        P("dm"),
        P("dm", "hv"),
        P(),
        P(),
    )
    return jax.shard_map(
        per_device, mesh=mesh, in_specs=placed, out_specs=(P(), P()), check_vma=False
    )
```

```python
import jax
import jax.numpy as jnp
from jax import lax
from jax.experimental import pallas as pl
from jax.experimental.pallas import tpu as pltpu
from jax.sharding import PartitionSpec as P

D = 16384
NZ, NC, NY, NX = 8, 2, 8, 4
ROWS = 16
WIDE = 1024
FF = 416
VOC = 1002
VPAD = 1024
CA = 384
CB = WIDE - CA
NH = 2
RH = ROWS // NH
OWN = 2 * RH
NOPT = 32
FAR8 = (4, 3, 5, 2, 6, 1, 7)
FAR4 = (2, 1, 3)
LOW = -1e30
COPIES = 240
GA, GB, SA, SB, SZ = False, False, False, False, True
MESH = pl.DeviceIdType.MESH
BF = jnp.bfloat16
F32 = jnp.float32
NT = (((1,), (1,)), ((), ()))


def kernel(
    tok_in, wg, wu, wd, gain_in, un, gold_in, lp_out,
    tok, gain, gold, w_in, w_gu, w_down, w_raw, w_un, w_lm, xa, xb, s1, r1, p1, s2, r2, hid,
    qa, qb, ra, rb, ta, tb, ra2, rb2, res, ya, yb,
    s3, r3, p3, s4, r4, st1, st3, send_sem, recv_sem, local_sem,
):
    dm = lax.axis_index("dm")
    hv = lax.axis_index("hv")
    z, c = dm // NC, lax.rem(dm, NC)
    y, x = hv // NX, lax.rem(hv, NX)
    oc = 1 - c

    def at(zz=None, cc=None, yy=None, xx=None):
        zz = z if zz is None else zz
        cc = c if cc is None else cc
        yy = y if yy is None else yy
        xx = x if xx is None else xx
        return (zz * NC + cc, yy * NX + xx)

    def up(v, k, n):
        return lax.rem(v + k, n)

    loads = [
        pltpu.make_async_copy(wg, w_in.at[pl.ds(0, FF)], local_sem.at[0]),
        pltpu.make_async_copy(wu, w_in.at[pl.ds(FF, FF)], local_sem.at[1]),
        pltpu.make_async_copy(wd, w_down, local_sem.at[2]),
        pltpu.make_async_copy(un, w_raw, local_sem.at[3]),
    ]
    small = [
        pltpu.make_async_copy(tok_in, tok, local_sem.at[4]),
        pltpu.make_async_copy(gain_in, gain, local_sem.at[5]),
        pltpu.make_async_copy(gold_in, gold, local_sem.at[6]),
    ]
    for load in small + loads:
        load.start()

    barrier = pltpu.get_barrier_semaphore()
    greet = (
        [at(yy=up(y, k, NY)) for k in FAR8]
        + [at(zz=up(z, k, NZ)) for k in FAR8]
        + [at(xx=up(x, k, NX)) for k in FAR4]
        + [at(cc=oc)]
    )
    for peer in greet:
        pl.semaphore_signal(barrier, inc=1, device_id=peer, device_id_type=MESH)
    for load in small:
        load.wait()
    pl.semaphore_wait(barrier, len(greet))

    count = [0]
    pending = []

    def send(src, dst, peer):
        n = count[0]
        count[0] = n + 1
        copy = pltpu.make_async_remote_copy(
            src_ref=src,
            dst_ref=dst,
            send_sem=send_sem.at[n],
            recv_sem=recv_sem.at[n],
            device_id=peer,
            device_id_type=MESH,
        )
        copy.start()
        pending.append(copy)
        return copy

    def sent(keep=0):
        done = pending[: len(pending) - keep]
        for copy in done:
            copy.wait_send()
        del pending[: len(done)]

    def arrive(copies):
        for copy in copies:
            copy.wait_recv()

    def cut(n):
        return n // 256 * 128

    def left(ref):
        most = (slice(None),) * (len(ref.shape) - 1)
        return ref.at[most + (pl.ds(0, cut(ref.shape[-1])),)]

    def right(ref):
        n = ref.shape[-1]
        most = (slice(None),) * (len(ref.shape) - 1)
        return ref.at[most + (pl.ds(cut(n), n - cut(n)),)]

    def spread_start(src, slot, p, peer, relay):
        return [send(src, slot(p), peer(k)) for k in ((2, 6, 1, 7) if relay else FAR8)]

    def spread_relay(first, slot, p, peer, relay):
        if not relay:
            return first
        arrive(first[:1])
        near = slot(up(p, 6, 8))
        more = [send(left(near), left(near), peer(2)), send(near, near, peer(1))]
        arrive(first[1:2])
        near = slot(up(p, 2, 8))
        more += [send(right(near), right(near), peer(6)), send(near, near, peer(7))]
        return first[2:] + more

    def sum_start(out, p, peer, got, relay):
        if not relay:
            return [send(out.at[up(p, k, 8)], got.at[i], peer(k)) for i, k in enumerate(FAR8)]
        far = out.at[up(p, 4, 8)]
        return [
            send(left(far), left(got.at[2]), peer(2)),
            send(right(far), right(got.at[2]), peer(6)),
            send(out.at[up(p, 3, 8)], got.at[0], peer(1)),
            send(out.at[up(p, 5, 8)], got.at[1], peer(7)),
            send(out.at[up(p, 1, 8)], got.at[5], peer(1)),
            send(out.at[up(p, 7, 8)], got.at[6], peer(7)),
        ]

    def sum_relay(first, out, p, peer, got, relay):
        if not relay:
            return first
        k = cut(out.shape[-1])
        arrive(first[:1] + first[2:3])
        term = out[up(p, 2, 8)].astype(F32) + got[0].astype(F32)
        got[3, ..., :k] = (term[..., :k] + got[2, ..., :k].astype(F32)).astype(BF)
        got[3, ..., k:] = term[..., k:].astype(BF)
        more = [send(got.at[3], got.at[7], peer(2))]
        arrive(first[1:2] + first[3:4])
        term = out[up(p, 6, 8)].astype(F32) + got[1].astype(F32)
        got[4, ..., k:] = (term[..., k:] + got[2, ..., k:].astype(F32)).astype(BF)
        got[4, ..., :k] = term[..., :k].astype(BF)
        more += [send(got.at[4], got.at[8], peer(6))]
        return first[4:] + more

    def sum_end(last, total, got, relay):
        spots = (5, 6, 7, 8) if relay else tuple(range(7))
        order = list(zip(spots, last))
        for i, copy in order if relay else reversed(order):
            arrive([copy])
            total = total + got[i].astype(F32)
        return total

    def along_y(k):
        return at(yy=up(y, k, NY))

    def along_z(k):
        return at(zz=up(z, k, NZ))

    def gather_hv(block_a, block_b, ga, gb):
        def slot_a(i):
            return ga.at[i]

        def slot_b(i):
            return gb.at[i, x]

        first_a = [send(block_a, ga.at[y, x], at(xx=up(x, k, NX))) for k in FAR4]
        first_b = spread_start(block_b, slot_b, y, along_y, GB)
        ga[y, x] = block_a[...]
        gb[y, x] = block_b[...]
        yield
        arrive(first_a)
        last = spread_start(ga.at[y], slot_a, y, along_y, GA)
        arrive(spread_relay(first_b, slot_b, y, along_y, GB))
        more = [send(gb.at[:, x], gb.at[:, x], at(xx=up(x, k, NX))) for k in FAR4]
        last = spread_relay(last, slot_a, y, along_y, GA)
        yield
        arrive(last + more)

    def part(ga, gb, cc):
        n = NY * 2 * RH
        a = ga[:, pl.ds(2 * cc, 2)].reshape(n, CA)
        b = gb[:, pl.ds(2 * cc, 2)].reshape(n, CB)
        return a, b

    def product(a, b, w):
        return jnp.dot(a, w[:CA, :], preferred_element_type=F32) + jnp.dot(
            b, w[CA:, :], preferred_element_type=F32
        )

    def scatter_dm(make, mine, out, got, out2, got2, done):
        out[...] = make(oc).astype(BF)
        swap = send(out, got, at(cc=oc))
        mine[...] = make(c)
        arrive([swap])
        out2[...] = (mine[...] + got[...].astype(F32)).astype(BF)
        copies = sum_start(out2, z, along_z, got2, SZ)
        total = mine[z] + got[z].astype(F32)
        yield
        copies = sum_relay(copies, out2, z, along_z, got2, SZ)
        if SZ:
            yield
        done.append(sum_end(copies, total, got2, SZ))

    def gate_up(cc, h):
        a, b = part(xa.at[h], xb.at[h], cc)
        return product(a, b, w_gu[...]).reshape(NZ, OWN, 2 * FF)

    def logit_part(cc, h):
        a, b = part(ya.at[h], yb.at[h], cc)
        out = product(a, b, w_lm[...])
        wide_a, wide_b = a.astype(F32), b.astype(F32)
        ss = jnp.sum(wide_a * wide_a, axis=1, keepdims=True) + jnp.sum(
            wide_b * wide_b, axis=1, keepdims=True
        )
        high = ss.astype(BF).astype(F32)
        tail = out[:, VPAD - 128 :]
        lane = lax.broadcasted_iota(jnp.int32, tail.shape, 1) + (VPAD - 128)
        tail = jnp.where(lane == VOC, high, jnp.where(lane == VOC + 1, ss - high, tail))
        out = jnp.concatenate([out[:, : VPAD - 128], tail], axis=1)
        return out.reshape(NZ, OWN, VPAD)

    def half(h, result):
        rows = pl.ds(h * RH, RH)
        yield from gather_hv(
            tok.at[rows, pl.ds(0, CA)], tok.at[rows, pl.ds(CA, CB)], xa.at[h], xb.at[h]
        )
        done = []
        yield from scatter_dm(
            lambda cc: gate_up(cc, h), p1.at[h], s1.at[h], r1.at[h], s2.at[h], r2.at[h], done
        )
        gate, upper = done[0][:, :FF], done[0][:, FF:]
        mine = hid.at[h]
        mine[z, c] = (gate / (1.0 + jnp.exp(-gate)) * upper).astype(BF)

        far = [send(mine.at[z, c], mine.at[z, c], at(zz=up(z, k, NZ))) for k in FAR8]
        near = [send(mine.at[z, c], mine.at[z, c], at(cc=oc))]
        yield
        for k, copy in reversed(list(zip(FAR8, far))):
            arrive([copy])
            origin = up(z, NZ - k, NZ)
            near.append(send(mine.at[origin, c], mine.at[origin, c], at(cc=oc)))
        arrive(near)

        q = jnp.dot(
            mine[...].reshape(NZ * NC * OWN, FF), w_down[...], preferred_element_type=F32
        )
        q = q.reshape(NY, NX, RH, WIDE).astype(BF)
        qa[h] = q[..., :CA]
        first_a = sum_start(qa.at[h], y, along_y, ra.at[h], SA)
        qb[h] = q[..., CA:]
        first_b = [
            send(qb.at[h, :, up(x, k, NX)], rb.at[h, i], at(xx=up(x, k, NX)))
            for i, k in enumerate(FAR4)
        ]
        yield
        first_a = sum_relay(first_a, qa.at[h], y, along_y, ra.at[h], SA)
        sum_b = qb[h, :, x].astype(F32)
        for i, copy in reversed(list(enumerate(first_b))):
            arrive([copy])
            sum_b = sum_b + rb[h, i].astype(F32)
        tb[h] = sum_b.astype(BF)
        last_b = sum_start(tb.at[h], y, along_y, rb2.at[h], SB)
        ta[h] = sum_end(first_a, qa[h, y].astype(F32), ra.at[h], SA).astype(BF)
        last_a = [
            send(ta.at[h, up(x, k, NX)], ra2.at[h, i], at(xx=up(x, k, NX)))
            for i, k in enumerate(FAR4)
        ]
        yield
        last_b = sum_relay(last_b, tb.at[h], y, along_y, rb2.at[h], SB)
        res_a = tok[rows, :CA].astype(F32) + ta[h, x].astype(F32)
        res_b = tok[rows, CA:].astype(F32) + tb[h, y].astype(F32)
        for i, copy in reversed(list(enumerate(last_a))):
            arrive([copy])
            res_a = res_a + ra2[h, i].astype(F32)
        res_b = sum_end(last_b, res_b, rb2.at[h], SB)
        res[h, :, :CA] = res_a.astype(BF)
        res[h, :, CA:] = res_b.astype(BF)

        yield from gather_hv(
            res.at[h, :, pl.ds(0, CA)], res.at[h, :, pl.ds(CA, CB)], ya.at[h], yb.at[h]
        )
        done = []
        yield from scatter_dm(
            lambda cc: logit_part(cc, h), p3.at[h], s3.at[h], r3.at[h], s4.at[h], r4.at[h], done
        )

        total = done[0]
        lane = lax.broadcasted_iota(jnp.int32, (OWN, VPAD), 1)
        ss = jnp.sum(
            jnp.where((lane == VOC) | (lane == VOC + 1), total, 0.0), axis=1, keepdims=True
        )
        logits = total * lax.rsqrt(ss / D + 1e-05)
        inside = lane < VOC
        top = jnp.max(jnp.where(inside, logits, LOW), axis=1, keepdims=True)
        mass = jnp.sum(jnp.where(inside, jnp.exp(logits - top), 0.0), axis=1, keepdims=True)
        row = lax.broadcasted_iota(jnp.int32, (OWN, 128), 0)
        col = lax.broadcasted_iota(jnp.int32, (OWN, 128), 1)
        spot = row // RH * ROWS + h * RH + lax.rem(row, RH) + lax.rem(dm, 4) * (2 * ROWS)
        diag = col == spot
        ids = gold[pl.ds(dm // 4, 1), :].astype(F32)
        wanted = jnp.sum(jnp.where(diag, ids, 0.0), axis=1, keepdims=True).astype(jnp.int32)
        hit = inside & (lane + hv * VOC == wanted)
        found = jnp.sum(jnp.where(hit, logits, 0.0), axis=1, keepdims=True)

        level = top + jnp.log(mass)
        other = col == lax.rem(spot + 2 * ROWS, 128)
        line = jnp.where(diag, level, jnp.where(other, found, 0.0))
        result.append(jnp.sum(line, axis=0, keepdims=True))

    def fold():
        g = gain[...]
        step = 32
        for load in loads:
            load.wait()
        w_gu[...] = w_in[...].T

        def some(i, carry):
            rows = pl.ds(pl.multiple_of(i * step, step), step)
            w_un[rows, :] = (w_raw[rows, :].astype(F32) * g).astype(BF)
            return carry

        whole = VOC // step
        lax.fori_loop(0, whole, some, 0)
        w_un[whole * step :, :] = jnp.zeros((VPAD - whole * step, WIDE), BF)
        w_un[whole * step : VOC, :] = (w_raw[whole * step :, :].astype(F32) * g).astype(BF)
        w_lm[...] = w_un[...].T

    results = []
    active = [half(h, results) for h in range(NH)]
    turn = 0
    while active:
        for walk in list(active):
            if next(walk, active) is active:
                active.remove(walk)
        if turn == 0:
            fold()
        turn += 1

    line = results[0]
    for t in results[1:]:
        line = line + t
    st1[hv] = line
    copies = [
        send(st1.at[hv], st1.at[hv], at(yy=up(y, j, NY), xx=up(x, k, NX)))
        for j in (4, 3, 5, 2, 6, 1, 7, 0)
        for k in (2, 1, 3, 0)
        if j or k
    ]
    sent(len(copies))
    arrive(copies)
    lines = [st1[i] for i in range(NY * NX)]
    best = lines[0]
    for t in lines[1:]:
        best = jnp.maximum(best, t)
    mass = jnp.zeros((1, 128), F32)
    found = jnp.zeros((1, 128), F32)
    for t in lines:
        mass = mass + jnp.exp(t - best)
        found = found + t
    level = best + jnp.log(mass)
    spot = lax.broadcasted_iota(jnp.int32, (1, 128), 1)
    base = lax.rem(dm, 4) * (2 * ROWS)
    valid = (spot >= base) & (spot < base + 2 * ROWS)
    st3[dm] = jnp.where(valid, pltpu.roll(found, 128 - 2 * ROWS, 1) - level, 0.0)
    copies = [
        send(st3.at[dm], st3.at[dm], at(zz=up(z, k, NZ), cc=up(c, e, NC)))
        for k in (4, 3, 5, 2, 6, 1, 7, 0)
        for e in (0, 1)
        if k or e
    ]
    sent(len(copies))
    arrive(copies)
    for i in range(4):
        lp_out[i : i + 1, :] = st3[4 * i] + st3[4 * i + 1] + st3[4 * i + 2] + st3[4 * i + 3]
    sent()


def options(lp, lens, lp_out, score_out):
    amount = lens[...].astype(F32)
    one = lax.broadcasted_iota(jnp.int32, (NOPT, NOPT), 0)
    two = lax.broadcasted_iota(jnp.int32, (NOPT, NOPT), 1)
    ends = jnp.sum(jnp.where(two <= one, amount, 0.0), axis=1, keepdims=True)
    length = jnp.sum(jnp.where(two == one, amount, 0.0), axis=1, keepdims=True)
    starts = ends - length
    col = lax.broadcasted_iota(jnp.int32, (NOPT, 128), 1)
    acc = jnp.zeros((NOPT, 1), F32)
    lp_out[...] = lp[...]
    for i in range(4):
        where = (col + 128 * i).astype(F32)
        member = (where >= starts) & (where < ends)
        acc = acc + jnp.sum(jnp.where(member, lp[i : i + 1, :], 0.0), axis=1, keepdims=True)
    score = acc / length
    score_out[...] = jnp.sum(jnp.where(two == one, score, 0.0), axis=0, keepdims=True)


def per_device(
    tokens, gate_weight, up_weight, down_weight, norm_gain, unembed, gold_ids, option_lengths
):
    vm = pl.BlockSpec(memory_space=pltpu.VMEM)
    anyspace = pl.BlockSpec(memory_space=pl.ANY)
    scratch = [
        pltpu.VMEM((ROWS, WIDE), BF),
        pltpu.VMEM((1, WIDE), F32),
        pltpu.VMEM((4, 128), jnp.int32),
        pltpu.VMEM((2 * FF, WIDE), BF),
        pltpu.VMEM((WIDE, 2 * FF), BF),
        pltpu.VMEM((FF, WIDE), BF),
        pltpu.VMEM((VOC, WIDE), BF),
        pltpu.VMEM((VPAD, WIDE), BF),
        pltpu.VMEM((WIDE, VPAD), BF),
        pltpu.VMEM((NH, NY, NX, RH, CA), BF),
        pltpu.VMEM((NH, NY, NX, RH, CB), BF),
        pltpu.VMEM((NH, NZ, OWN, 2 * FF), BF),
        pltpu.VMEM((NH, NZ, OWN, 2 * FF), BF),
        pltpu.VMEM((NH, NZ, OWN, 2 * FF), F32),
        pltpu.VMEM((NH, NZ, OWN, 2 * FF), BF),
        pltpu.VMEM((NH, 9, OWN, 2 * FF), BF),
        pltpu.VMEM((NH, NZ, NC, OWN, FF), BF),
        pltpu.VMEM((NH, NY, NX, RH, CA), BF),
        pltpu.VMEM((NH, NY, NX, RH, CB), BF),
        pltpu.VMEM((NH, 9, NX, RH, CA), BF),
        pltpu.VMEM((NH, NX - 1, NY, RH, CB), BF),
        pltpu.VMEM((NH, NX, RH, CA), BF),
        pltpu.VMEM((NH, NY, RH, CB), BF),
        pltpu.VMEM((NH, NX - 1, RH, CA), BF),
        pltpu.VMEM((NH, 9, RH, CB), BF),
        pltpu.VMEM((NH, RH, WIDE), BF),
        pltpu.VMEM((NH, NY, NX, RH, CA), BF),
        pltpu.VMEM((NH, NY, NX, RH, CB), BF),
        pltpu.VMEM((NH, NZ, OWN, VPAD), BF),
        pltpu.VMEM((NH, NZ, OWN, VPAD), BF),
        pltpu.VMEM((NH, NZ, OWN, VPAD), F32),
        pltpu.VMEM((NH, NZ, OWN, VPAD), BF),
        pltpu.VMEM((NH, 9, OWN, VPAD), BF),
        pltpu.VMEM((NY * NX, 1, 128), F32),
        pltpu.VMEM((NZ * NC, 1, 128), F32),
        pltpu.SemaphoreType.DMA((COPIES,)),
        pltpu.SemaphoreType.DMA((COPIES,)),
        pltpu.SemaphoreType.DMA((7,)),
    ]
    raw = pl.pallas_call(
        kernel,
        out_shape=jax.ShapeDtypeStruct((4, 128), F32),
        in_specs=[anyspace] * 7,
        out_specs=vm,
        scratch_shapes=scratch,
        name="score",
        compiler_params=pltpu.CompilerParams(
            collective_id=0, has_side_effects=True, vmem_limit_bytes=56 << 20
        ),
    )(
        tokens,
        gate_weight.T,
        up_weight.T,
        down_weight,
        norm_gain.reshape(1, WIDE),
        unembed.T,
        gold_ids.reshape(4, 128),
    )
    logprob, score = pl.pallas_call(
        options,
        out_shape=(
            jax.ShapeDtypeStruct((4, 128), F32),
            jax.ShapeDtypeStruct((1, NOPT), F32),
        ),
        in_specs=[vm, vm],
        out_specs=(vm, vm),
        name="options",
    )(raw, option_lengths.reshape(1, NOPT))
    return logprob.reshape(512), score.reshape(NOPT)


def solution(mesh):
    placed = (
        P("hv", "dm"),
        P("dm", "hv"),
        P("dm", "hv"),
        P("hv", "dm"),
        P("dm"),
        P("dm", "hv"),
        P(),
        P(),
    )
    return jax.shard_map(
        per_device, mesh=mesh, in_specs=placed, out_specs=(P(), P()), check_vma=False
    )
```
